256 devices in a mesh: ctx: 32 (over x, y, core), head: 8 (over z).
Axes of the slice: x: 4, y: 4, z: 8, core: 2. Of those that a mesh axis runs over, the one named last changes fastest.
Arguments:
- lin_q: bfloat16 [4096, 8192], P('ctx', 'head'), may hold values from -5 to 5
- lin_k: bfloat16 [4096, 8192], P('ctx', 'head'), may hold values from -5 to 5
- lin_v: bfloat16 [4096, 8192], P('ctx', 'head'), may hold values from -52 to 52
- log_decay: float32 [4096, 64], P('ctx', 'head'), may hold values from -1.5 to 0
- norm_gain: float32 [8192], P('head'), may hold values from 0.25 to 1.75
- lin_cot: bfloat16 [4096, 8192], P('ctx', 'head'), may hold values from -5 to 5
- soft_q: bfloat16 [4096, 8192], P('ctx', 'head'), may hold values from -5 to 5
- soft_k: bfloat16 [4096, 1024], P('ctx', 'head'), may hold values from -5 to 5
- soft_v: bfloat16 [4096, 1024], P('ctx', 'head'), may hold values from -5 to 5
- soft_cot: bfloat16 [4096, 8192], P('ctx', 'head'), may hold values from -5 to 5
Outputs:
- lin_dq: float32 [4096, 8192], P('ctx', 'head')
- lin_dk: float32 [4096, 8192], P('ctx', 'head')
- lin_dv: float32 [4096, 8192], P('ctx', 'head')
- gain_grad: float32 [8192], P('head')
- soft_dq: float32 [4096, 8192], P('ctx', 'head')
- soft_dk: float32 [4096, 1024], P('ctx', 'head')
- soft_dv: float32 [4096, 1024], P('ctx', 'head')
The draws below stay inside these ranges and needn't reach their ends.
All inputs are finite; a program needn't handle non-finite values.
Results may differ from the reference program's by a relative error of at most 0.018.
Values may be sent and summed in bfloat16 or wider, within the bound.
A program may use at most 128 MiB of HBM per device.

```python
import jax
import jax.numpy as jnp
from jax import lax

HEAD_DIM = 128
LINEAR_HEADS = 64
SOFT_HEADS = 64
KV_HEADS = 8
TOK_DEV = 128
SEQUENCE_LENGTH = 4096
GROUP = 8


def draw_lin_v(key, part):
    feat_width = LINEAR_HEADS * HEAD_DIM
    head_frac = (jnp.arange(feat_width) // HEAD_DIM).astype(jnp.float32) / max(LINEAR_HEADS - 1, 1)
    jitter = jax.random.uniform(jax.random.fold_in(key, 2), (feat_width,), jnp.float32, 0.7, 1.3)
    base_rows = jnp.clip(jax.random.normal(jax.random.fold_in(key, 1), (SEQUENCE_LENGTH, feat_width), jnp.float32), -4.0, 4.0)
    factor = 10.0 ** head_frac
    return (base_rows * (factor * jitter)[None, :]).astype(jnp.bfloat16)


def draw_log_decay(key, part):
    blocks = SEQUENCE_LENGTH // TOK_DEV
    fast_share = 0.5
    picks = jax.random.uniform(jax.random.fold_in(key, 1), (LINEAR_HEADS,), jnp.float32)
    baseline_rate = jnp.where(picks < fast_share, 0.025, 0.5 / SEQUENCE_LENGTH)
    block_multiplier = jnp.exp(jax.random.uniform(jax.random.fold_in(key, 2), (blocks, LINEAR_HEADS), jnp.float32, jnp.log(0.6), jnp.log(1.6)))
    block_multiplier = jnp.repeat(block_multiplier, TOK_DEV, axis=0)
    coarse_estimate = jax.random.uniform(jax.random.fold_in(key, 3), (SEQUENCE_LENGTH, LINEAR_HEADS), jnp.float32, 0.5, 1.5)
    spike_position = jax.random.randint(jax.random.fold_in(key, 4), (2, LINEAR_HEADS), 0, SEQUENCE_LENGTH)
    spike_penalty = jax.random.uniform(jax.random.fold_in(key, 5), (2, LINEAR_HEADS), jnp.float32, 0.2, 0.5)
    position_list = jnp.arange(SEQUENCE_LENGTH)[:, None]
    spike_events = jnp.where(position_list == spike_position[0][None, :], jnp.log(1.0 - spike_penalty[0])[None, :], 0.0)
    spike_events = spike_events + jnp.where(position_list == spike_position[1][None, :], jnp.log(1.0 - spike_penalty[1])[None, :], 0.0)
    return -baseline_rate[None, :] * block_multiplier * coarse_estimate + spike_events


def draw_soft_q(key, part):
    base_rows = jnp.clip(jax.random.normal(jax.random.fold_in(key, 3), (SEQUENCE_LENGTH, SOFT_HEADS * HEAD_DIM), jnp.float32), -4.0, 4.0)
    return base_rows.astype(jnp.bfloat16)


def draw_soft_k(key, part):
    base_rows = jnp.clip(jax.random.normal(jax.random.fold_in(key, 4), (SEQUENCE_LENGTH, KV_HEADS * HEAD_DIM), jnp.float32), -4.0, 4.0)
    return base_rows.astype(jnp.bfloat16)


def shard_levels(stream_key, shape, pieces, low, top_value):
    gain = 1.0
    for dim, parts in pieces:
        steps = jax.random.uniform(jax.random.fold_in(jax.random.fold_in(stream_key, 6), dim), (parts,), jnp.float32, low / len(pieces), top_value / len(pieces))
        gain = gain * jnp.repeat(jnp.exp(steps), shape[dim] // parts).reshape((-1,) + (1,) * (len(shape) - 1 - dim))
    return gain


def bell_draw(own_key, shape, spread, bound, pieces=(), kind=jnp.bfloat16):
    gain = shard_levels(own_key, shape, pieces, -0.22, 0.18) if pieces else 1.0
    values = jax.random.normal(own_key, shape, jnp.float32) * spread * gain
    return jnp.minimum(jnp.maximum(values, -bound), bound).astype(kind)


def setup_inputs(seed: int = 0) -> dict:
    arg_keys = jax.random.split(jax.random.key(seed), 11)
    lin_q = bell_draw(arg_keys[0], (SEQUENCE_LENGTH, LINEAR_HEADS * HEAD_DIM), 1.0, 5.0, ((0, 32), (1, 8)))
    lin_k = bell_draw(arg_keys[1], (SEQUENCE_LENGTH, LINEAR_HEADS * HEAD_DIM), 1.0, 5.0, ((0, 32), (1, 8)))
    lin_v = draw_lin_v(jax.random.fold_in(arg_keys[10], 71), 0)
    log_decay = draw_log_decay(jax.random.fold_in(arg_keys[10], 71), 0)
    norm_gain = jnp.clip(1.0 + 0.15 * jax.random.normal(arg_keys[4], (LINEAR_HEADS * HEAD_DIM,), jnp.float32), 0.25, 1.75)
    lin_cot = bell_draw(arg_keys[5], (SEQUENCE_LENGTH, LINEAR_HEADS * HEAD_DIM), 1.0, 5.0, ((0, 32), (1, 8)))
    soft_q = draw_soft_q(jax.random.fold_in(arg_keys[10], 71), 0)
    soft_k = draw_soft_k(jax.random.fold_in(arg_keys[10], 71), 0)
    soft_v = bell_draw(arg_keys[8], (SEQUENCE_LENGTH, KV_HEADS * HEAD_DIM), 1.0, 5.0, ((0, 32), (1, 8)))
    soft_cot = bell_draw(arg_keys[9], (SEQUENCE_LENGTH, SOFT_HEADS * HEAD_DIM), 1.0, 5.0, ((0, 32), (1, 8)))
    return dict(lin_q=lin_q, lin_k=lin_k, lin_v=lin_v, log_decay=log_decay, norm_gain=norm_gain, lin_cot=lin_cot, soft_q=soft_q, soft_k=soft_k, soft_v=soft_v, soft_cot=soft_cot)


EPS = 1e-06
NEG = -1e+30

def rounded(values):
    return lax.optimization_barrier(values.astype(jnp.bfloat16)).astype(jnp.float32)

def lightning_grads(lin_q, lin_k, lin_v, log_decay, norm_gain, lin_cot):
    score_scale = HEAD_DIM ** (-0.5)
    blocks = SEQUENCE_LENGTH // TOK_DEV
    shape_four = (blocks, TOK_DEV, LINEAR_HEADS, HEAD_DIM)
    queries = lin_q.reshape(shape_four).astype(jnp.float32)
    key_rows = lin_k.reshape(shape_four).astype(jnp.float32)
    values = lin_v.reshape(shape_four).astype(jnp.float32)
    log_cum = jnp.cumsum(log_decay.reshape(blocks, TOK_DEV, LINEAR_HEADS), axis=1)
    decay_total = log_cum[:, -1]
    key_decay = jnp.exp(decay_total[:, None, :] - log_cum)
    query_decay = jnp.exp(log_cum)
    keys_dec = rounded(key_rows * key_decay[..., None])
    queries_dec = rounded(queries * query_decay[..., None])
    local_states = jnp.einsum('bthd,bthe->bhde', keys_dec, values)
    zero_state = jnp.zeros((LINEAR_HEADS, HEAD_DIM, HEAD_DIM), jnp.float32)

    def forward_step(running, scan_item):
        decay_sum, local_term = scan_item
        return (jnp.exp(decay_sum)[:, None, None] * running + local_term, running)
    _, entering = lax.scan(forward_step, zero_state, (decay_total, local_states))
    entering = rounded(entering)
    offsets = jnp.arange(TOK_DEV, dtype=jnp.int32)
    causal = offsets[None, :] <= offsets[:, None]
    log_gap = log_cum[:, :, None, :] - log_cum[:, None, :, :]
    decay_mat = jnp.where(causal[None, :, :, None], jnp.exp(jnp.minimum(log_gap, 0.0)), 0.0)
    decay_mat = jnp.transpose(decay_mat, (0, 3, 1, 2))
    weights = rounded(jnp.einsum('bthd,bshd->bhts', queries, key_rows) * score_scale * decay_mat)
    output = jnp.einsum('bhts,bshe->bthe', weights, values) + score_scale * query_decay[..., None] * jnp.einsum('bthd,bhde->bthe', queries, entering)
    feat_width = LINEAR_HEADS * HEAD_DIM
    flat_out = output.reshape(SEQUENCE_LENGTH, feat_width)
    inv_rms = lax.rsqrt(lax.optimization_barrier(jnp.sum(flat_out * flat_out, axis=1)) / feat_width + EPS)
    normed = flat_out * inv_rms[:, None]
    cot_rows = lin_cot.astype(jnp.float32)
    scaled_cot = cot_rows * norm_gain[None, :]
    mean_cross = lax.optimization_barrier(jnp.sum(scaled_cot * normed, axis=1)) / feat_width
    out_cot = rounded((scaled_cot - normed * mean_cross[:, None]) * inv_rms[:, None])
    gain_grad = lax.optimization_barrier(jnp.sum(cot_rows * normed, axis=0))
    out_cot = out_cot.reshape(shape_four)
    local_grads = jnp.einsum('bthd,bthe->bhde', queries_dec, out_cot)

    def backward_step(running, scan_item):
        decay_sum, local_term = scan_item
        return (local_term + jnp.exp(decay_sum)[:, None, None] * running, running)
    _, after = lax.scan(backward_step, zero_state, (decay_total, local_grads), reverse=True)
    after = rounded(after)
    dweights = rounded(jnp.einsum('bthe,bshe->bhts', out_cot, values) * score_scale * decay_mat)
    grad_q = jnp.einsum('bhts,bshd->bthd', dweights, key_rows) + score_scale * query_decay[..., None] * jnp.einsum('bthe,bhde->bthd', out_cot, entering)
    grad_k = jnp.einsum('bhts,bthd->bshd', dweights, queries) + score_scale * key_decay[..., None] * jnp.einsum('bshe,bhde->bshd', values, after)
    grad_v = jnp.einsum('bhts,bthe->bshe', weights, out_cot) + score_scale * key_decay[..., None] * jnp.einsum('bshd,bhde->bshe', key_rows, after)
    return (grad_q.reshape(SEQUENCE_LENGTH, feat_width), grad_k.reshape(SEQUENCE_LENGTH, feat_width), grad_v.reshape(SEQUENCE_LENGTH, feat_width), gain_grad)

def softmax_grads(soft_q, soft_k, soft_v, soft_cot):
    score_scale = HEAD_DIM ** (-0.5)
    blocks = SEQUENCE_LENGTH // TOK_DEV
    queries = soft_q.reshape(blocks, TOK_DEV, KV_HEADS, GROUP, HEAD_DIM).astype(jnp.float32)
    cot_rows = soft_cot.reshape(blocks, TOK_DEV, KV_HEADS, GROUP, HEAD_DIM).astype(jnp.float32)
    key_rows = soft_k.reshape(blocks, TOK_DEV, KV_HEADS, HEAD_DIM).astype(jnp.float32)
    values = soft_v.reshape(blocks, TOK_DEV, KV_HEADS, HEAD_DIM).astype(jnp.float32)
    offsets = jnp.arange(TOK_DEV, dtype=jnp.int32)
    block_ids = jnp.arange(blocks, dtype=jnp.int32)

    def block_scores(query_block, key_block, query_index, key_index):
        scores = jnp.einsum('tkgd,nkd->kgtn', query_block, key_block) * score_scale
        allowed = (key_index * TOK_DEV + offsets)[None, :] <= (query_index * TOK_DEV + offsets)[:, None]
        return (scores, allowed)

    def forward_block(query_index):
        query_block = queries[query_index]

        def visit(running, key_index):

            def update(inner):
                run_max, run_sum, run_acc = inner
                scores, allowed = block_scores(query_block, key_rows[key_index], query_index, key_index)
                block_max = lax.optimization_barrier(jnp.max(jnp.where(allowed, scores, NEG), axis=-1))
                new_max = jnp.maximum(run_max, block_max)
                probs = jnp.exp(jnp.where(allowed, scores - new_max[..., None], NEG))
                factor = jnp.exp(run_max - new_max)
                run_sum = run_sum * factor + lax.optimization_barrier(jnp.sum(probs, axis=-1))
                run_acc = run_acc * factor[..., None] + jnp.einsum('kgtn,nkd->kgtd', probs, values[key_index], precision=lax.Precision.HIGHEST)
                return (new_max, run_sum, run_acc)
            return (lax.cond(key_index <= query_index, update, lambda inner: inner, running), None)
        start_state = (jnp.full((KV_HEADS, GROUP, TOK_DEV), NEG, jnp.float32), jnp.zeros((KV_HEADS, GROUP, TOK_DEV), jnp.float32), jnp.zeros((KV_HEADS, GROUP, TOK_DEV, HEAD_DIM), jnp.float32))
        (run_max, run_sum, run_acc), _ = lax.scan(visit, start_state, block_ids)
        log_sum = run_max + jnp.log(run_sum)
        attn_out = run_acc / run_sum[..., None]
        delta = lax.optimization_barrier(jnp.sum(jnp.transpose(cot_rows[query_index], (1, 2, 0, 3)) * attn_out, axis=-1))
        return (log_sum, delta)
    log_sums, deltas = lax.map(forward_block, block_ids)

    def grad_block(running, query_index):
        query_block = queries[query_index]
        cot_block = cot_rows[query_index]
        log_sum = log_sums[query_index]
        delta = deltas[query_index]

        def visit(inner_state, key_index):

            def update(inner):
                q_grad, key_acc, value_acc = inner
                key_block = key_rows[key_index]
                value_block = values[key_index]
                scores, allowed = block_scores(query_block, key_block, query_index, key_index)
                probs = jnp.exp(jnp.where(allowed, scores - log_sum[..., None], NEG))
                dprobs = jnp.einsum('tkgd,nkd->kgtn', cot_block, value_block)
                dscores = rounded(probs * (dprobs - delta[..., None]) * score_scale)
                q_grad = q_grad + jnp.einsum('kgtn,nkd->kgtd', dscores, key_block)
                key_acc = key_acc.at[key_index].add(jnp.einsum('kgtn,tkgd->nkd', dscores, query_block))
                value_acc = value_acc.at[key_index].add(jnp.einsum('kgtn,tkgd->nkd', rounded(probs), cot_block))
                return (q_grad, key_acc, value_acc)
            return (lax.cond(key_index <= query_index, update, lambda inner: inner, inner_state), None)
        key_acc, value_acc = running
        start_grad = jnp.zeros((KV_HEADS, GROUP, TOK_DEV, HEAD_DIM), jnp.float32)
        (q_grad, key_acc, value_acc), _ = lax.scan(visit, (start_grad, key_acc, value_acc), block_ids)
        return ((key_acc, value_acc), q_grad)
    zero_keys = jnp.zeros((blocks, TOK_DEV, KV_HEADS, HEAD_DIM), jnp.float32)
    (key_acc, value_acc), q_grads = lax.scan(grad_block, (zero_keys, zero_keys), block_ids)
    soft_dq = jnp.transpose(q_grads, (0, 3, 1, 2, 4)).reshape(SEQUENCE_LENGTH, SOFT_HEADS * HEAD_DIM)
    return (soft_dq, key_acc.reshape(SEQUENCE_LENGTH, KV_HEADS * HEAD_DIM), value_acc.reshape(SEQUENCE_LENGTH, KV_HEADS * HEAD_DIM))

def reference(lin_q, lin_k, lin_v, log_decay, norm_gain, lin_cot, soft_q, soft_k, soft_v, soft_cot):
    lin_dq, lin_dk, lin_dv, gain_grad = lightning_grads(lin_q, lin_k, lin_v, log_decay, norm_gain, lin_cot)
    soft_dq, soft_dk, soft_dv = softmax_grads(soft_q, soft_k, soft_v, soft_cot)
    return (lin_dq, lin_dk, lin_dv, gain_grad, soft_dq, soft_dk, soft_dv)
```

```python
import functools
import math

import jax
import jax.numpy as jnp
from jax import lax
from jax.experimental import pallas as pl
from jax.experimental.pallas import tpu as pltpu
from jax.sharding import PartitionSpec as P

D = 128
H = 8
EPS = 1e-06
NEG = -1e30
SCALE = D**-0.5
LOG2E = math.log2(math.e)
F32 = jnp.float32
BF16 = jnp.bfloat16
HIGH = lax.Precision.HIGHEST
MESH = pl.DeviceIdType.MESH


def dot(a, b, ca=1, cb=0, precision=None):
    return lax.dot_general(
        a, b, (((ca,), (cb,)), ((), ())), precision=precision, preferred_element_type=F32
    )


def hs(h):
    return slice(h * D, (h + 1) * D)


def column(row):
    return jnp.broadcast_to(row, (D, D)).T


def kernel(
    n, nh,
    lq, lk, lv, ld, gain, lc, sq, sk, sv, sc,
    o_dq, o_dk, o_dv, o_gg, o_sdq, o_sdk, o_sdv,
    sbuf, dpbuf, kv, pbuf, prec, osend, orec,
    qt, ct, qr, cr, dscb, pb, dqt, m8, l8, d8,
    ms, pw, out, dout, lsend, lrec, esend, erec, wsend, wrec, asend, arec,
    dec, decs, ggs, ggr, pss, psr,
    a2a_s, a2a_r, kv_s, kv_r, pr_s, pr_r, os_s, os_r,
):
    me = lax.axis_index("ctx")
    hd = lax.axis_index("head")
    chip = me // 2
    core = me % 2
    partner = me + 1 - 2 * core
    nc = n // 2
    spn = n // H
    rs = D // spn
    width = H * D

    barrier = pltpu.get_barrier_semaphore()

    @pl.loop(1, n)
    def _(d):
        pl.semaphore_signal(
            barrier, inc=1, device_id={"ctx": lax.rem(me + d, n)}, device_id_type=MESH
        )

    @pl.loop(1, nh)
    def _(d):
        pl.semaphore_signal(
            barrier, inc=1, device_id={"head": lax.rem(hd + d, nh)}, device_id_type=MESH
        )

    kv[chip, core, 0] = sk[...]
    kv[chip, core, 1] = sv[...]

    row_i = lax.broadcasted_iota(jnp.int32, (D, D), 0)
    col_i = lax.broadcasted_iota(jnp.int32, (D, D), 1)
    causal = col_i <= row_i
    tri = jnp.where(causal, 1.0, 0.0).astype(F32)
    ldv = ld[...]
    cum = dot(tri, ldv, 1, 0, HIGH)
    cum_t = dot(ldv, tri, 0, 1, HIGH)
    kdec = jnp.exp(cum[D - 1 : D, :] - cum)
    qdec = jnp.exp(cum)
    tot_t = jnp.exp(cum_t[:, D - 1 : D])

    def col(a, h):
        return jnp.broadcast_to(a[:, h : h + 1], (D, D))

    for h in range(H):
        kd = (lk[:, hs(h)].astype(F32) * col(kdec, h)).astype(BF16)
        local = dot(kd, lv[:, hs(h)], 0, 0)
        lsend[h * spn : (h + 1) * spn] = local.astype(BF16).reshape(spn, rs, D)
        dec[h] = jnp.broadcast_to(tot_t[h : h + 1, :], (1, D))
    lrec[me] = lsend[me]
    decs[me] = dec[me // spn]

    pl.semaphore_wait(barrier, n - 1 + nh - 1)

    def exchange(src, dst, k, by_target=True, pick=None):
        @pl.loop(1, n)
        def _(d):
            to = lax.rem(me + d, n)
            if pick is not None:
                s = src.at[pick(to)]
            else:
                s = src.at[to] if by_target else src
            pltpu.make_async_remote_copy(
                src_ref=s,
                dst_ref=dst.at[me],
                send_sem=a2a_s.at[k],
                recv_sem=a2a_r.at[k],
                device_id={"ctx": to},
                device_id_type=MESH,
            ).start()

    def arrived(dst, k, count):
        part = dst.at[pl.ds(0, count)]
        pltpu.make_async_copy(part, part, a2a_r.at[k]).wait()

    def left(dst, k, count):
        part = dst.at[pl.ds(0, count)]
        pltpu.make_async_copy(part, part, a2a_s.at[k]).wait()

    exchange(lsend, lrec, 0)
    exchange(dec, decs, 1, pick=lambda to: to // spn)

    def kv_copy(k, par, sem, to):
        return pltpu.make_async_remote_copy(
            src_ref=kv.at[k, par],
            dst_ref=kv.at[k, par],
            send_sem=kv_s.at[sem],
            recv_sem=kv_r.at[k, par],
            device_id={"ctx": to},
            device_id_type=MESH,
        )

    def kv_send():
        kv_copy(chip, core, chip, partner).start()

        @pl.loop(chip + 1, nc)
        def _(k):
            kv_copy(chip, core, k, 2 * k + core).start()

    def kv_wait(k, par):
        part = kv.at[k, par]
        pltpu.make_async_copy(part, part, kv_r.at[k, par]).wait()

    def kv_relay():
        @pl.loop(0, chip)
        def _(i):
            k = chip - 1 - i
            kv_wait(k, core)
            kv_copy(k, core, k, partner).start()

    kv_send()

    for h in range(H):
        gap = col(cum, h) - jnp.broadcast_to(cum_t[h : h + 1, :], (D, D))
        m = jnp.where(causal, jnp.exp(jnp.minimum(gap, 0.0)), 0.0) * SCALE
        ms[h] = m
        p = (dot(lq[:, hs(h)], lk[:, hs(h)], 1, 1) * m).astype(BF16)
        pw[h] = p
        out[:, hs(h)] = dot(p, lv[:, hs(h)])

    m8[...] = jnp.full((8, width), NEG, F32)
    for h in range(H):
        qh = sq[:, hs(h)]
        chh = sc[:, hs(h)]
        qt[:, hs(h)] = qh.T
        ct[:, hs(h)] = chh.T

    arrived(lrec, 0, n - 1)
    arrived(decs, 1, n - 1)
    run = jnp.zeros((rs, D), F32)
    for c in range(n):
        esend[c] = run.astype(BF16)
        run = jnp.broadcast_to(decs[c], (rs, D)) * run + lrec[c].astype(F32)
    erec[me] = esend[me]
    exchange(esend, erec, 2)

    kv_relay()

    def scores(k, masked):
        keys = kv[k, :, 0].reshape(2 * D, D)
        vals = kv[k, :, 1].reshape(2 * D, D)
        for j in range(width // 256):
            lanes = slice(j * 256, (j + 1) * 256)
            s = dot(keys, qt[:, lanes])
            if masked:
                kpos = lax.broadcasted_iota(jnp.int32, (2 * D, 256), 0)
                qpos = core * D + lax.broadcasted_iota(jnp.int32, (2 * D, 256), 1) % D
                s = jnp.where(kpos <= qpos, s, NEG)
            sbuf[k, :, lanes] = s
            m8[:, lanes] = jnp.maximum(m8[:, lanes], jnp.max(s.reshape(2 * D // 8, 8, 256), axis=0))
            dpbuf[k, :, lanes] = dot(vals, ct[:, lanes])

    kv_wait(chip, 1 - core)
    scores(chip, True)

    arrived(erec, 2, n - 1)

    def state(ref, h):
        return ref[h * spn : (h + 1) * spn].reshape(D, D)

    sum_sq = jnp.zeros((D, D), F32)
    sum_x = jnp.zeros((D, D), F32)
    for h in range(H):
        o = out[:, hs(h)] + (SCALE * col(qdec, h)) * dot(lq[:, hs(h)], state(erec, h))
        out[:, hs(h)] = o
        sum_sq += o * o
        sum_x += lc[:, hs(h)].astype(F32) * gain[:, hs(h)] * o
    ones = jnp.ones((8, D), F32)
    pss[0] = dot(ones, sum_sq, 1, 1, HIGH)
    pss[1] = dot(ones, sum_x, 1, 1, HIGH)
    psr[hd] = pss[...]

    @pl.loop(1, nh)
    def _(d):
        to = lax.rem(hd + d, nh)
        pltpu.make_async_remote_copy(
            src_ref=pss,
            dst_ref=psr.at[hd],
            send_sem=a2a_s.at[3],
            recv_sem=a2a_r.at[3],
            device_id={"head": to},
            device_id_type=MESH,
        ).start()

    @pl.loop(0, chip // 2)
    def _(i):
        k = chip - 1 - i
        kv_wait(k, 1 - core)
        scores(k, False)

    arrived(psr, 3, nh - 1)
    sums = jnp.sum(psr[...], axis=0)
    inv = lax.rsqrt(sums[0, 0:1] / (nh * width) + EPS)
    cross = sums[1, 0:1] * inv / (nh * width)
    inv_c = column(inv)
    cross_c = column(cross)
    for h in range(H):
        normed = out[:, hs(h)] * inv_c
        cot = lc[:, hs(h)].astype(F32)
        do = ((cot * gain[:, hs(h)] - normed * cross_c) * inv_c).astype(BF16)
        dout[:, hs(h)] = do
        ggs[h : h + 1, :] = jnp.sum(cot * normed, axis=0, keepdims=True)
        qd = (lq[:, hs(h)].astype(F32) * col(qdec, h)).astype(BF16)
        wsend[h * spn : (h + 1) * spn] = dot(qd, do, 0, 0).astype(BF16).reshape(spn, rs, D)
    wrec[me] = wsend[me]
    ggr[me] = ggs[...]
    exchange(wsend, wrec, 4)
    exchange(ggs, ggr, 5, by_target=False)

    for h in range(H):
        do = dout[:, hs(h)]
        dp = (dot(do, lv[:, hs(h)], 1, 1) * ms[h]).astype(BF16)
        o_dq[:, hs(h)] = dot(dp, lk[:, hs(h)]) + (SCALE * col(qdec, h)) * dot(do, state(erec, h), 1, 1)
        o_dk[:, hs(h)] = dot(dp, lq[:, hs(h)], 0, 0)
        o_dv[:, hs(h)] = dot(pw[h], do, 0, 0)

    arrived(wrec, 4, n - 1)
    run = jnp.zeros((rs, D), F32)
    for c in range(n - 1, -1, -1):
        asend[c] = run.astype(BF16)
        run = jnp.broadcast_to(decs[c], (rs, D)) * run + wrec[c].astype(F32)
    arec[me] = asend[me]
    exchange(asend, arec, 6)

    @pl.loop(chip // 2, chip)
    def _(i):
        k = chip - 1 - i
        kv_wait(k, 1 - core)
        scores(k, False)

    factor = SCALE * LOG2E
    top = jnp.max(m8[...], axis=0, keepdims=True) * factor
    l8[...] = jnp.zeros((8, width), F32)
    d8[...] = jnp.zeros((8, width), F32)

    @pl.loop(0, chip + 1)
    def _(k):
        for j in range(width // 256):
            lanes = slice(j * 256, (j + 1) * 256)
            p = jnp.exp2(sbuf[k, :, lanes] * factor - top[:, lanes])
            sbuf[k, :, lanes] = p
            l8[:, lanes] += jnp.sum(p.reshape(2 * D // 8, 8, 256), axis=0)
            d8[:, lanes] += jnp.sum((p * dpbuf[k, :, lanes]).reshape(2 * D // 8, 8, 256), axis=0)

    rinv = 1.0 / jnp.sum(l8[...], axis=0, keepdims=True)
    delta = jnp.sum(d8[...], axis=0, keepdims=True) * rinv
    for h in range(H):
        rc = column(rinv[:, hs(h)])
        qr[h * D : (h + 1) * D, :] = (sq[:, hs(h)].astype(F32) * (rc * SCALE)).astype(BF16)
        cr[h * D : (h + 1) * D, :] = (sc[:, hs(h)].astype(F32) * rc).astype(BF16)

    arrived(arec, 6, n - 1)
    for h in range(H):
        a = state(arec, h)
        kd = SCALE * col(kdec, h)
        o_dk[:, hs(h)] += kd * dot(lv[:, hs(h)], a, 1, 1)
        o_dv[:, hs(h)] += kd * dot(lk[:, hs(h)], a)

    dqt[...] = jnp.zeros((D, width), F32)

    def pair_copy(k):
        return pltpu.make_async_remote_copy(
            src_ref=pbuf.at[k, 1 - core],
            dst_ref=prec.at[k],
            send_sem=pr_s.at[k],
            recv_sem=pr_r.at[k],
            device_id={"ctx": partner},
            device_id_type=MESH,
        )

    def own_copy(k):
        return pltpu.make_async_remote_copy(
            src_ref=osend.at[k],
            dst_ref=orec.at[chip],
            send_sem=os_s.at[k],
            recv_sem=os_r.at[chip],
            device_id={"ctx": 2 * k + core},
            device_id_type=MESH,
        )

    def own_send(k):
        pltpu.make_async_copy(prec.at[k], prec.at[k], pr_r.at[k]).wait()
        osend[k] = (pbuf[k, core].astype(F32) + prec[k].astype(F32)).astype(BF16)
        own_copy(k).start()

    @pl.loop(0, chip + 1)
    def _(k):
        keys = kv[k, :, 0].reshape(2 * D, D)
        for j in range(width // 256):
            lanes = slice(j * 256, (j + 1) * 256)
            p = sbuf[k, :, lanes]
            pb[:, lanes] = p.astype(BF16)
            ds = (p * (dpbuf[k, :, lanes] - delta[:, lanes])).astype(BF16)
            dscb[:, lanes] = ds
            dqt[:, lanes] += dot(keys, ds, 0, 0)
        dk = dot(dscb[...], qr[...])
        dv = dot(pb[...], cr[...])
        pbuf[k, :, 0] = dk.astype(BF16).reshape(2, D, D)
        pbuf[k, :, 1] = dv.astype(BF16).reshape(2, D, D)
        pair_copy(k).start()

        @pl.when(k > 0)
        def _():
            own_send(k - 1)

    for h in range(H):
        o_sdq[:, hs(h)] = (dqt[:, hs(h)] * (rinv[:, hs(h)] * SCALE)).T

    arrived(ggr, 5, n - 1)
    o_gg[...] = jnp.sum(ggr[...], axis=0)

    pltpu.make_async_copy(prec.at[chip], prec.at[chip], pr_r.at[chip]).wait()
    o_sdk[...] = pbuf[chip, core, 0].astype(F32) + prec[chip, 0].astype(F32)
    o_sdv[...] = pbuf[chip, core, 1].astype(F32) + prec[chip, 1].astype(F32)

    @pl.loop(chip + 1, nc)
    def _(k):
        pltpu.make_async_copy(orec.at[k], orec.at[k], os_r.at[k]).wait()
        o_sdk[...] += orec[k, 0].astype(F32)
        o_sdv[...] += orec[k, 1].astype(F32)

    left(lsend, 0, n - 1)
    left(decs, 1, n - 1)
    left(esend, 2, n - 1)
    left(psr, 3, nh - 1)
    left(wsend, 4, n - 1)
    left(ggr, 5, n - 1)
    left(asend, 6, n - 1)

    @pl.loop(0, nc)
    def _(k):
        pltpu.make_async_copy(kv.at[0, 0], kv.at[0, 0], kv_s.at[k]).wait()

    @pl.loop(0, chip + 1)
    def _(k):
        pltpu.make_async_copy(prec.at[k], prec.at[k], pr_s.at[k]).wait()

    @pl.loop(0, chip)
    def _(k):
        pltpu.make_async_copy(osend.at[k], osend.at[k], os_s.at[k]).wait()


def on_device(n, nh, lq, lk, lv, ld, gain, lc, sq, sk, sv, sc):
    nc = n // 2
    spn = n // H
    rs = D // spn
    width = H * D
    state = pltpu.VMEM((n, rs, D), BF16)
    scratch = [
        pltpu.VMEM((nc, 2 * D, width), F32),
        pltpu.VMEM((nc, 2 * D, width), F32),
        pltpu.VMEM((nc, 2, 2, D, D), BF16),
        pltpu.VMEM((nc, 2, 2, D, D), BF16),
        pltpu.VMEM((nc, 2, D, D), BF16),
        pltpu.VMEM((nc, 2, D, D), BF16),
        pltpu.VMEM((nc, 2, D, D), BF16),
        pltpu.VMEM((D, width), BF16),
        pltpu.VMEM((D, width), BF16),
        pltpu.VMEM((width, D), BF16),
        pltpu.VMEM((width, D), BF16),
        pltpu.VMEM((2 * D, width), BF16),
        pltpu.VMEM((2 * D, width), BF16),
        pltpu.VMEM((D, width), F32),
        pltpu.VMEM((8, width), F32),
        pltpu.VMEM((8, width), F32),
        pltpu.VMEM((8, width), F32),
        pltpu.VMEM((H, D, D), F32),
        pltpu.VMEM((H, D, D), BF16),
        pltpu.VMEM((D, width), F32),
        pltpu.VMEM((D, width), BF16),
        *([state] * 8),
        pltpu.VMEM((H, 1, D), F32),
        pltpu.VMEM((n, 1, D), F32),
        pltpu.VMEM((H, D), F32),
        pltpu.VMEM((n, H, D), F32),
        pltpu.VMEM((2, 8, D), F32),
        pltpu.VMEM((nh, 2, 8, D), F32),
        pltpu.SemaphoreType.DMA((7,)),
        pltpu.SemaphoreType.DMA((7,)),
        pltpu.SemaphoreType.DMA((nc,)),
        pltpu.SemaphoreType.DMA((nc, 2)),
        pltpu.SemaphoreType.DMA((nc,)),
        pltpu.SemaphoreType.DMA((nc,)),
        pltpu.SemaphoreType.DMA((nc,)),
        pltpu.SemaphoreType.DMA((nc,)),
    ]
    big = jax.ShapeDtypeStruct((D, width), F32)
    small = jax.ShapeDtypeStruct((D, D), F32)
    vmem = pl.BlockSpec(memory_space=pltpu.VMEM)
    res = pl.pallas_call(
        functools.partial(kernel, n, nh),
        out_shape=(big, big, big, jax.ShapeDtypeStruct((H, D), F32), big, small, small),
        in_specs=[vmem] * 10,
        out_specs=(vmem,) * 7,
        scratch_shapes=scratch,
        compiler_params=pltpu.CompilerParams(
            collective_id=0, has_side_effects=True, vmem_limit_bytes=62 * 1024 * 1024
        ),
        name="grads",
    )(lq, lk, lv, ld, gain.reshape(1, width), lc, sq, sk, sv, sc)
    dq, dk, dv, gg, sdq, sdk, sdv = res
    return dq, dk, dv, gg.reshape(width), sdq, sdk, sdv


def solution(mesh):
    n, nh = mesh.shape["ctx"], mesh.shape["head"]
    both = P("ctx", "head")
    return jax.shard_map(
        functools.partial(on_device, n, nh),
        mesh=mesh,
        in_specs=(both, both, both, both, P("head"), both, both, both, both, both),
        out_specs=(both, both, both, P("head"), both, both, both),
        check_vma=False,
    )
```

```python
import functools
import math

import jax
import jax.numpy as jnp
from jax import lax
from jax.experimental import pallas as pl
from jax.experimental.pallas import tpu as pltpu
from jax.sharding import PartitionSpec as P

D = 128
H = 8
EPS = 1e-06
NEG = -1e30
SCALE = D**-0.5
LOG2E = math.log2(math.e)
F32 = jnp.float32
BF16 = jnp.bfloat16
HIGH = lax.Precision.HIGHEST
MESH = pl.DeviceIdType.MESH


def dot(a, b, ca=1, cb=0, precision=None):
    return lax.dot_general(
        a, b, (((ca,), (cb,)), ((), ())), precision=precision, preferred_element_type=F32
    )


def hs(h):
    return slice(h * D, (h + 1) * D)


def column(row):
    return jnp.broadcast_to(row, (D, D)).T


def kernel(
    n, nh, gy,
    lq, lk, lv, ld, gain, lc, sq, sk, sv, sc,
    o_dq, o_dk, o_dv, o_gg, o_sdq, o_sdk, o_sdv,
    sbuf, dpbuf, kv, pbuf, prec, osend, orec, xsend, xrec, acc,
    qt, ct, qr, cr, dscb, pb, dqt, m8, l8, d8,
    ms, pw, out, dout, lsend, lrec, esend, erec, wsend, wrec, asend, arec,
    dec, decs, ggs, ggr, pss, psr,
    a2a_s, a2a_r, kv_s, kv_f, kv_r, pr_s, pr_r, os_s, os_r, xs_s, xs_r,
):
    me = lax.axis_index("ctx")
    hd = lax.axis_index("head")
    chip = me // 2
    core = me % 2
    partner = me + 1 - 2 * core
    nc = n // 2
    gx = nc // gy
    cx, cy = chip // gy, chip % gy
    spn = n // H
    rs = D // spn
    width = H * D

    barrier = pltpu.get_barrier_semaphore()

    @pl.loop(1, n)
    def _(d):
        pl.semaphore_signal(
            barrier, inc=1, device_id={"ctx": lax.rem(me + d, n)}, device_id_type=MESH
        )

    @pl.loop(1, nh)
    def _(d):
        pl.semaphore_signal(
            barrier, inc=1, device_id={"head": lax.rem(hd + d, nh)}, device_id_type=MESH
        )

    kv[chip, core, 0] = sk[...]
    kv[chip, core, 1] = sv[...]

    row_i = lax.broadcasted_iota(jnp.int32, (D, D), 0)
    col_i = lax.broadcasted_iota(jnp.int32, (D, D), 1)
    causal = col_i <= row_i
    tri = jnp.where(causal, 1.0, 0.0).astype(F32)
    ldv = ld[...]
    cum = dot(tri, ldv, 1, 1, HIGH)
    cum_t = dot(ldv, tri, 1, 1, HIGH)
    kdec = jnp.exp(cum[D - 1 : D, :] - cum)
    qdec = jnp.exp(cum)
    tot_t = jnp.exp(cum_t[:, D - 1 : D])

    def col(a, h):
        return jnp.broadcast_to(a[:, h : h + 1], (D, D))

    for h in range(H):
        kd = (lk[:, hs(h)].astype(F32) * col(kdec, h)).astype(BF16)
        local = dot(kd, lv[:, hs(h)], 0, 0)
        lsend[h * spn : (h + 1) * spn] = local.astype(BF16).reshape(spn, rs, D)
        dec[h] = jnp.broadcast_to(tot_t[h : h + 1, :], (1, D))
    lrec[me] = lsend[me]
    decs[me] = dec[me // spn]

    pl.semaphore_wait(barrier, n - 1 + nh - 1)

    def exchange(src, dst, k, by_target=True, pick=None):
        @pl.loop(1, n)
        def _(d):
            to = lax.rem(me + d, n)
            if pick is not None:
                s = src.at[pick(to)]
            else:
                s = src.at[to] if by_target else src
            pltpu.make_async_remote_copy(
                src_ref=s,
                dst_ref=dst.at[me],
                send_sem=a2a_s.at[k],
                recv_sem=a2a_r.at[k],
                device_id={"ctx": to},
                device_id_type=MESH,
            ).start()

    def arrived(dst, k, count):
        part = dst.at[pl.ds(0, count)]
        pltpu.make_async_copy(part, part, a2a_r.at[k]).wait()

    def left(dst, k, count):
        part = dst.at[pl.ds(0, count)]
        pltpu.make_async_copy(part, part, a2a_s.at[k]).wait()

    exchange(lsend, lrec, 0)
    exchange(dec, decs, 1, pick=lambda to: to // spn)

    def kv_copy(k, sem, to):
        return pltpu.make_async_remote_copy(
            src_ref=kv.at[k, core],
            dst_ref=kv.at[k, core],
            send_sem=sem,
            recv_sem=kv_r.at[k, core],
            device_id={"ctx": to},
            device_id_type=MESH,
        )

    def kv_send():
        kv_copy(chip, kv_s.at[chip], partner).start()

        @pl.loop(cx + 1, gx)
        def _(x):
            k = x * gy + cy
            kv_copy(chip, kv_f.at[k], 2 * k + core).start()

        @pl.loop(cy + 1, gy)
        def _(y):
            k = cx * gy + y
            kv_copy(chip, kv_f.at[k], 2 * k + core).start()

    def kv_spread():
        @pl.loop(0, cx)
        def _(i):
            x = cx - 1 - i
            k = x * gy + cy
            kv_wait(k, core)

            @pl.loop(1, gy)
            def _(d):
                y = lax.rem(cy + d, gy)
                kv_copy(k, kv_f.at[x * gy + y], 2 * (cx * gy + y) + core).start()

            kv_copy(k, kv_s.at[k], partner).start()

    def kv_wait(k, par):
        part = kv.at[k, par]
        pltpu.make_async_copy(part, part, kv_r.at[k, par]).wait()

    def kv_relay():
        @pl.loop(0, chip)
        def _(i):
            k = chip - 1 - i

            @pl.when(k % gy != cy)
            def _():
                kv_wait(k, core)
                kv_copy(k, kv_s.at[k], partner).start()

    kv_send()

    for h in range(H):
        gap = col(cum, h) - jnp.broadcast_to(cum_t[h : h + 1, :], (D, D))
        m = jnp.where(causal, jnp.exp(jnp.minimum(gap, 0.0)), 0.0) * SCALE
        ms[h] = m
        p = (dot(lq[:, hs(h)], lk[:, hs(h)], 1, 1) * m).astype(BF16)
        pw[h] = p
        out[:, hs(h)] = dot(p, lv[:, hs(h)])

    m8[...] = jnp.full((8, width), NEG, F32)
    for h in range(H):
        qh = sq[:, hs(h)]
        chh = sc[:, hs(h)]
        qt[:, hs(h)] = qh.T
        ct[:, hs(h)] = chh.T

    arrived(lrec, 0, n - 1)
    arrived(decs, 1, n - 1)
    run = jnp.zeros((rs, D), F32)
    for c in range(n):
        esend[c] = run.astype(BF16)
        run = jnp.broadcast_to(decs[c], (rs, D)) * run + lrec[c].astype(F32)
    erec[me] = esend[me]
    exchange(esend, erec, 2)
    kv_spread()

    def scores(k, masked):
        keys = kv[k, :, 0].reshape(2 * D, D)
        vals = kv[k, :, 1].reshape(2 * D, D)
        for j in range(width // 256):
            lanes = slice(j * 256, (j + 1) * 256)
            s = dot(keys, qt[:, lanes])
            if masked:
                kpos = lax.broadcasted_iota(jnp.int32, (2 * D, 256), 0)
                qpos = core * D + lax.broadcasted_iota(jnp.int32, (2 * D, 256), 1) % D
                s = jnp.where(kpos <= qpos, s, NEG)
            sbuf[k, :, lanes] = s
            m8[:, lanes] = jnp.maximum(m8[:, lanes], jnp.max(s.reshape(2 * D // 8, 8, 256), axis=0))
            dpbuf[k, :, lanes] = dot(vals, ct[:, lanes])

    kv_wait(chip, 1 - core)
    scores(chip, True)

    arrived(erec, 2, n - 1)

    def state(ref, h):
        return ref[h * spn : (h + 1) * spn].reshape(D, D)

    sum_sq = jnp.zeros((D, D), F32)
    sum_x = jnp.zeros((D, D), F32)
    for h in range(H):
        o = out[:, hs(h)] + (SCALE * col(qdec, h)) * dot(lq[:, hs(h)], state(erec, h))
        out[:, hs(h)] = o
        sum_sq += o * o
        sum_x += lc[:, hs(h)].astype(F32) * gain[:, hs(h)] * o
    ones = jnp.ones((8, D), F32)
    pss[0] = dot(ones, sum_sq, 1, 1, HIGH)
    pss[1] = dot(ones, sum_x, 1, 1, HIGH)
    psr[hd] = pss[...]

    @pl.loop(1, nh)
    def _(d):
        to = lax.rem(hd + d, nh)
        pltpu.make_async_remote_copy(
            src_ref=pss,
            dst_ref=psr.at[hd],
            send_sem=a2a_s.at[3],
            recv_sem=a2a_r.at[3],
            device_id={"head": to},
            device_id_type=MESH,
        ).start()

    kv_relay()

    @pl.loop(0, chip // 2)
    def _(i):
        k = chip - 1 - i
        kv_wait(k, 1 - core)
        scores(k, False)

    arrived(psr, 3, nh - 1)
    sums = jnp.sum(psr[...], axis=0)
    inv = lax.rsqrt(sums[0, 0:1] / (nh * width) + EPS)
    cross = sums[1, 0:1] * inv / (nh * width)
    inv_c = column(inv)
    cross_c = column(cross)
    for h in range(H):
        normed = out[:, hs(h)] * inv_c
        cot = lc[:, hs(h)].astype(F32)
        do = ((cot * gain[:, hs(h)] - normed * cross_c) * inv_c).astype(BF16)
        dout[:, hs(h)] = do
        ggs[h : h + 1, :] = jnp.sum(cot * normed, axis=0, keepdims=True)
        qd = (lq[:, hs(h)].astype(F32) * col(qdec, h)).astype(BF16)
        wsend[h * spn : (h + 1) * spn] = dot(qd, do, 0, 0).astype(BF16).reshape(spn, rs, D)
    wrec[me] = wsend[me]
    ggr[me] = ggs[...]
    exchange(wsend, wrec, 4)
    exchange(ggs, ggr, 5, by_target=False)

    for h in range(H):
        do = dout[:, hs(h)]
        dp = (dot(do, lv[:, hs(h)], 1, 1) * ms[h]).astype(BF16)
        o_dq[:, hs(h)] = dot(dp, lk[:, hs(h)]) + (SCALE * col(qdec, h)) * dot(do, state(erec, h), 1, 1)
        o_dk[:, hs(h)] = dot(dp, lq[:, hs(h)], 0, 0)
        o_dv[:, hs(h)] = dot(pw[h], do, 0, 0)

    arrived(wrec, 4, n - 1)
    run = jnp.zeros((rs, D), F32)
    for c in range(n - 1, -1, -1):
        asend[c] = run.astype(BF16)
        run = jnp.broadcast_to(decs[c], (rs, D)) * run + wrec[c].astype(F32)
    arec[me] = asend[me]
    exchange(asend, arec, 6)

    @pl.loop(chip // 2, chip)
    def _(i):
        k = chip - 1 - i
        kv_wait(k, 1 - core)
        scores(k, False)

    factor = SCALE * LOG2E
    top = jnp.max(m8[...], axis=0, keepdims=True) * factor
    l8[...] = jnp.zeros((8, width), F32)
    d8[...] = jnp.zeros((8, width), F32)

    @pl.loop(0, chip + 1)
    def _(k):
        for j in range(width // 256):
            lanes = slice(j * 256, (j + 1) * 256)
            p = jnp.exp2(sbuf[k, :, lanes] * factor - top[:, lanes])
            sbuf[k, :, lanes] = p
            l8[:, lanes] += jnp.sum(p.reshape(2 * D // 8, 8, 256), axis=0)
            d8[:, lanes] += jnp.sum((p * dpbuf[k, :, lanes]).reshape(2 * D // 8, 8, 256), axis=0)

    rinv = 1.0 / jnp.sum(l8[...], axis=0, keepdims=True)
    delta = jnp.sum(d8[...], axis=0, keepdims=True) * rinv
    for h in range(H):
        rc = column(rinv[:, hs(h)])
        qr[h * D : (h + 1) * D, :] = (sq[:, hs(h)].astype(F32) * (rc * SCALE)).astype(BF16)
        cr[h * D : (h + 1) * D, :] = (sc[:, hs(h)].astype(F32) * rc).astype(BF16)

    arrived(arec, 6, n - 1)
    for h in range(H):
        a = state(arec, h)
        kd = SCALE * col(kdec, h)
        o_dk[:, hs(h)] += kd * dot(lv[:, hs(h)], a, 1, 1)
        o_dv[:, hs(h)] += kd * dot(lk[:, hs(h)], a)

    dqt[...] = jnp.zeros((D, width), F32)

    def pair_copy(k):
        return pltpu.make_async_remote_copy(
            src_ref=pbuf.at[k, 1 - core],
            dst_ref=prec.at[k],
            send_sem=pr_s.at[k],
            recv_sem=pr_r.at[k],
            device_id={"ctx": partner},
            device_id_type=MESH,
        )

    def y_copy(k):
        x, y = k // gy, k % gy
        return pltpu.make_async_remote_copy(
            src_ref=osend.at[k],
            dst_ref=orec.at[x, cy],
            send_sem=os_s.at[k],
            recv_sem=os_r.at[x, cy],
            device_id={"ctx": 2 * (cx * gy + y) + core},
            device_id_type=MESH,
        )

    def x_copy(x):
        return pltpu.make_async_remote_copy(
            src_ref=xsend.at[x],
            dst_ref=xrec.at[cx],
            send_sem=xs_s.at[x],
            recv_sem=xs_r.at[cx],
            device_id={"ctx": 2 * (x * gy + cy) + core},
            device_id_type=MESH,
        )

    def own_send(k):
        pltpu.make_async_copy(prec.at[k], prec.at[k], pr_r.at[k]).wait()
        osend[k] = (pbuf[k, core].astype(F32) + prec[k].astype(F32)).astype(BF16)

        @pl.when(k % gy != cy)
        def _():
            y_copy(k).start()

    @pl.loop(0, chip + 1)
    def _(k):
        keys = kv[k, :, 0].reshape(2 * D, D)
        for j in range(width // 256):
            lanes = slice(j * 256, (j + 1) * 256)
            p = sbuf[k, :, lanes]
            pb[:, lanes] = p.astype(BF16)
            ds = (p * (dpbuf[k, :, lanes] - delta[:, lanes])).astype(BF16)
            dscb[:, lanes] = ds
            dqt[:, lanes] += dot(keys, ds, 0, 0)
        dk = dot(dscb[...], qr[...])
        dv = dot(pb[...], cr[...])
        pbuf[k, :, 0] = dk.astype(BF16).reshape(2, D, D)
        pbuf[k, :, 1] = dv.astype(BF16).reshape(2, D, D)
        pair_copy(k).start()

        @pl.when(k > 0)
        def _():
            own_send(k - 1)

    for h in range(H):
        o_sdq[:, hs(h)] = (dqt[:, hs(h)] * (rinv[:, hs(h)] * SCALE)).T

    arrived(ggr, 5, n - 1)
    o_gg[...] = jnp.sum(ggr[...], axis=0)

    def y_add(x, y):
        pltpu.make_async_copy(orec.at[x, y], orec.at[x, y], os_r.at[x, y]).wait()
        acc[...] += orec[x, y].astype(F32)

    @pl.loop(0, cx)
    def _(x):
        acc[...] = osend[x * gy + cy].astype(F32)

        @pl.loop(1, gy)
        def _(d):
            y_add(x, lax.rem(cy + d, gy))

        xsend[x] = acc[...].astype(BF16)
        x_copy(x).start()

    pltpu.make_async_copy(prec.at[chip], prec.at[chip], pr_r.at[chip]).wait()
    acc[...] = pbuf[chip, core].astype(F32) + prec[chip].astype(F32)

    @pl.loop(cy + 1, gy)
    def _(y):
        y_add(cx, y)

    @pl.loop(cx + 1, gx)
    def _(x):
        pltpu.make_async_copy(xrec.at[x], xrec.at[x], xs_r.at[x]).wait()
        acc[...] += xrec[x].astype(F32)

    o_sdk[...] = acc[0]
    o_sdv[...] = acc[1]

    left(lsend, 0, n - 1)
    left(decs, 1, n - 1)
    left(esend, 2, n - 1)
    left(psr, 3, nh - 1)
    left(wsend, 4, n - 1)
    left(ggr, 5, n - 1)
    left(asend, 6, n - 1)

    @pl.loop(0, nc)
    def _(k):
        @pl.when(k <= chip)
        def _():
            pltpu.make_async_copy(kv.at[0, 0], kv.at[0, 0], kv_s.at[k]).wait()

        x, y = k // gy, k % gy
        sent = ((x < cx) & (y != cy)) | ((x == cx) & (y > cy)) | ((x > cx) & (y == cy))

        @pl.when(sent)
        def _():
            pltpu.make_async_copy(kv.at[0, 0], kv.at[0, 0], kv_f.at[k]).wait()

    @pl.loop(0, chip + 1)
    def _(k):
        pltpu.make_async_copy(prec.at[k], prec.at[k], pr_s.at[k]).wait()

    @pl.loop(0, chip)
    def _(k):
        @pl.when(k % gy != cy)
        def _():
            pltpu.make_async_copy(osend.at[k], osend.at[k], os_s.at[k]).wait()

    @pl.loop(0, cx)
    def _(x):
        pltpu.make_async_copy(xsend.at[x], xsend.at[x], xs_s.at[x]).wait()


def finish(*refs):
    copies = [pltpu.make_async_copy(refs[i], refs[7 + i], refs[14].at[i]) for i in range(7)]
    for copy in copies:
        copy.start()
    for copy in copies:
        copy.wait()


def on_device(n, nh, lq, lk, lv, ld, gain, lc, sq, sk, sv, sc):
    nc = n // 2
    gy = math.isqrt(nc)
    gx = nc // gy
    spn = n // H
    rs = D // spn
    width = H * D
    state = pltpu.VMEM((n, rs, D), BF16)
    scratch = [
        pltpu.VMEM((nc, 2 * D, width), F32),
        pltpu.VMEM((nc, 2 * D, width), F32),
        pltpu.VMEM((nc, 2, 2, D, D), BF16),
        pltpu.VMEM((nc, 2, 2, D, D), BF16),
        pltpu.VMEM((nc, 2, D, D), BF16),
        pltpu.VMEM((nc, 2, D, D), BF16),
        pltpu.VMEM((gx, gy, 2, D, D), BF16),
        pltpu.VMEM((gx, 2, D, D), BF16),
        pltpu.VMEM((gx, 2, D, D), BF16),
        pltpu.VMEM((2, D, D), F32),
        pltpu.VMEM((D, width), BF16),
        pltpu.VMEM((D, width), BF16),
        pltpu.VMEM((width, D), BF16),
        pltpu.VMEM((width, D), BF16),
        pltpu.VMEM((2 * D, width), BF16),
        pltpu.VMEM((2 * D, width), BF16),
        pltpu.VMEM((D, width), F32),
        pltpu.VMEM((8, width), F32),
        pltpu.VMEM((8, width), F32),
        pltpu.VMEM((8, width), F32),
        pltpu.VMEM((H, D, D), F32),
        pltpu.VMEM((H, D, D), BF16),
        pltpu.VMEM((D, width), F32),
        pltpu.VMEM((D, width), BF16),
        *([state] * 8),
        pltpu.VMEM((H, 1, D), F32),
        pltpu.VMEM((n, 1, D), F32),
        pltpu.VMEM((H, D), F32),
        pltpu.VMEM((n, H, D), F32),
        pltpu.VMEM((2, 8, D), F32),
        pltpu.VMEM((nh, 2, 8, D), F32),
        pltpu.SemaphoreType.DMA((7,)),
        pltpu.SemaphoreType.DMA((7,)),
        pltpu.SemaphoreType.DMA((nc,)),
        pltpu.SemaphoreType.DMA((nc,)),
        pltpu.SemaphoreType.DMA((nc, 2)),
        pltpu.SemaphoreType.DMA((nc,)),
        pltpu.SemaphoreType.DMA((nc,)),
        pltpu.SemaphoreType.DMA((nc,)),
        pltpu.SemaphoreType.DMA((gx, gy)),
        pltpu.SemaphoreType.DMA((gx,)),
        pltpu.SemaphoreType.DMA((gx,)),
    ]
    big = jax.ShapeDtypeStruct((D, width), F32)
    small = jax.ShapeDtypeStruct((D, D), F32)
    vmem = pl.BlockSpec(memory_space=pltpu.VMEM)
    res = pl.pallas_call(
        functools.partial(kernel, n, nh, gy),
        out_shape=(big, big, big, jax.ShapeDtypeStruct((H, D), F32), big, small, small),
        in_specs=[vmem] * 10,
        out_specs=(vmem,) * 7,
        scratch_shapes=scratch,
        compiler_params=pltpu.CompilerParams(
            collective_id=0, has_side_effects=True, vmem_limit_bytes=48 * 1024 * 1024
        ),
        name="grads",
    )(lq, lk, lv, ld.T, gain.reshape(1, width), lc, sq, sk, sv, sc)
    dq, dk, dv, gg, sdq, sdk, sdv = pl.pallas_call(
        finish,
        out_shape=tuple(jax.ShapeDtypeStruct(r.shape, r.dtype) for r in res),
        in_specs=[vmem] * 7,
        out_specs=(pl.BlockSpec(memory_space=pl.ANY),) * 7,
        scratch_shapes=[pltpu.SemaphoreType.DMA((7,))],
        compiler_params=pltpu.CompilerParams(vmem_limit_bytes=8 * 1024 * 1024),
        name="finish",
    )(*res)
    return dq, dk, dv, gg.reshape(width), sdq, sdk, sdv


def solution(mesh):
    n, nh = mesh.shape["ctx"], mesh.shape["head"]
    both = P("ctx", "head")
    return jax.shard_map(
        functools.partial(on_device, n, nh),
        mesh=mesh,
        in_specs=(both, both, both, both, P("head"), both, both, both, both, both),
        out_specs=(both, both, both, P("head"), both, both, both),
        check_vma=False,
    )
```

```python
import functools
import math

import jax
import jax.numpy as jnp
from jax import lax
from jax.experimental import pallas as pl
from jax.experimental.pallas import tpu as pltpu
from jax.sharding import PartitionSpec as P

D = 128
H = 8
EPS = 1e-06
NEG = -1e30
SCALE = D**-0.5
LOG2E = math.log2(math.e)
F32 = jnp.float32
BF16 = jnp.bfloat16
HIGH = lax.Precision.HIGHEST
MESH = pl.DeviceIdType.MESH


def dot(a, b, ca=1, cb=0, precision=None):
    return lax.dot_general(
        a, b, (((ca,), (cb,)), ((), ())), precision=precision, preferred_element_type=F32
    )


def hs(h):
    return slice(h * D, (h + 1) * D)


def column(row):
    return jnp.broadcast_to(row, (D, D)).T


def kernel(
    n, nh, gy,
    lq_h, lk_h, lv_h, ld_h, gain_h, lc_h, sq_h, sk_h, sv_h, sc_h,
    o_dq, o_dk, o_dv, o_gg, o_sdq, o_sdk, o_sdv,
    sbuf, dpbuf, kv, pbuf, prec, osend, orec, xsend, xrec, acc,
    qt, ct, qr, cr, dscb, pb, dqt, m8, l8, d8,
    ms, pw, out, dout, lsend, lrec, esend, erec, wsend, wrec, asend, arec,
    dec, decs, ggs, ggr, pss, psr, lq, lk, lv, ld, gain, lc, sq, sc, in_s,
    a2a_s, a2a_r, kv_s, kv_f, kv_r, pr_s, pr_r, os_s, os_r, xs_s, xs_r,
):
    me = lax.axis_index("ctx")
    hd = lax.axis_index("head")
    chip = me // 2
    core = me % 2
    partner = me + 1 - 2 * core
    nc = n // 2
    gx = nc // gy
    cx, cy = chip // gy, chip % gy
    spn = n // H
    rs = D // spn
    width = H * D

    loads = [
        pltpu.make_async_copy(a, b, in_s.at[i])
        for i, (a, b) in enumerate(
            [
                (ld_h, ld),
                (lk_h, lk),
                (lv_h, lv),
                (sk_h, kv.at[chip, core, 0]),
                (sv_h, kv.at[chip, core, 1]),
                (lq_h, lq),
                (sq_h, sq),
                (sc_h, sc),
                (lc_h, lc),
                (gain_h, gain),
            ]
        )
    ]
    for load in loads:
        load.start()

    barrier = pltpu.get_barrier_semaphore()

    @pl.loop(1, n)
    def _(d):
        pl.semaphore_signal(
            barrier, inc=1, device_id={"ctx": lax.rem(me + d, n)}, device_id_type=MESH
        )

    @pl.loop(1, nh)
    def _(d):
        pl.semaphore_signal(
            barrier, inc=1, device_id={"head": lax.rem(hd + d, nh)}, device_id_type=MESH
        )

    row_i = lax.broadcasted_iota(jnp.int32, (D, D), 0)
    col_i = lax.broadcasted_iota(jnp.int32, (D, D), 1)
    causal = col_i <= row_i
    tri = jnp.where(causal, 1.0, 0.0).astype(F32)
    loads[0].wait()
    ldv = ld[...]
    cum = dot(tri, ldv, 1, 1, HIGH)
    cum_t = dot(ldv, tri, 1, 1, HIGH)
    kdec = jnp.exp(cum[D - 1 : D, :] - cum)
    qdec = jnp.exp(cum)
    tot_t = jnp.exp(cum_t[:, D - 1 : D])

    def col(a, h):
        return jnp.broadcast_to(a[:, h : h + 1], (D, D))

    loads[1].wait()
    loads[2].wait()
    for h in range(H):
        kd = (lk[:, hs(h)].astype(F32) * col(kdec, h)).astype(BF16)
        local = dot(kd, lv[:, hs(h)], 0, 0)
        lsend[h * spn : (h + 1) * spn] = local.astype(BF16).reshape(spn, rs, D)
        dec[h] = jnp.broadcast_to(tot_t[h : h + 1, :], (1, D))
    lrec[me] = lsend[me]
    decs[me] = dec[me // spn]

    for load in loads[3:]:
        load.wait()
    pl.semaphore_wait(barrier, n - 1 + nh - 1)

    def exchange(src, dst, k, by_target=True, pick=None):
        @pl.loop(1, n)
        def _(d):
            to = lax.rem(me + d, n)
            if pick is not None:
                s = src.at[pick(to)]
            else:
                s = src.at[to] if by_target else src
            pltpu.make_async_remote_copy(
                src_ref=s,
                dst_ref=dst.at[me],
                send_sem=a2a_s.at[k],
                recv_sem=a2a_r.at[k],
                device_id={"ctx": to},
                device_id_type=MESH,
            ).start()

    def arrived(dst, k, count):
        part = dst.at[pl.ds(0, count)]
        pltpu.make_async_copy(part, part, a2a_r.at[k]).wait()

    def left(dst, k, count):
        part = dst.at[pl.ds(0, count)]
        pltpu.make_async_copy(part, part, a2a_s.at[k]).wait()

    exchange(lsend, lrec, 0)
    exchange(dec, decs, 1, pick=lambda to: to // spn)

    def kv_copy(k, sem, to):
        return pltpu.make_async_remote_copy(
            src_ref=kv.at[k, core],
            dst_ref=kv.at[k, core],
            send_sem=sem,
            recv_sem=kv_r.at[k, core],
            device_id={"ctx": to},
            device_id_type=MESH,
        )

    def kv_send():
        kv_copy(chip, kv_s.at[chip], partner).start()

        @pl.loop(cx + 1, gx)
        def _(x):
            k = x * gy + cy
            kv_copy(chip, kv_f.at[k], 2 * k + core).start()

        @pl.loop(cy + 1, gy)
        def _(y):
            k = cx * gy + y
            kv_copy(chip, kv_f.at[k], 2 * k + core).start()

    def kv_spread():
        @pl.loop(0, cx)
        def _(i):
            x = cx - 1 - i
            k = x * gy + cy
            kv_wait(k, core)

            @pl.loop(1, gy)
            def _(d):
                y = lax.rem(cy + d, gy)
                kv_copy(k, kv_f.at[x * gy + y], 2 * (cx * gy + y) + core).start()

            kv_copy(k, kv_s.at[k], partner).start()

    def kv_wait(k, par):
        part = kv.at[k, par]
        pltpu.make_async_copy(part, part, kv_r.at[k, par]).wait()

    def kv_relay():
        @pl.loop(0, chip)
        def _(i):
            k = chip - 1 - i

            @pl.when(k % gy != cy)
            def _():
                kv_wait(k, core)
                kv_copy(k, kv_s.at[k], partner).start()

    kv_send()

    for h in range(H):
        gap = col(cum, h) - jnp.broadcast_to(cum_t[h : h + 1, :], (D, D))
        m = jnp.where(causal, jnp.exp(jnp.minimum(gap, 0.0)), 0.0) * SCALE
        ms[h] = m
        p = (dot(lq[:, hs(h)], lk[:, hs(h)], 1, 1) * m).astype(BF16)
        pw[h] = p
        out[:, hs(h)] = dot(p, lv[:, hs(h)])

    m8[...] = jnp.full((8, width), NEG, F32)
    for h in range(H):
        qh = sq[:, hs(h)]
        chh = sc[:, hs(h)]
        qt[:, hs(h)] = qh.T
        ct[:, hs(h)] = chh.T

    arrived(lrec, 0, n - 1)
    arrived(decs, 1, n - 1)
    run = jnp.zeros((rs, D), F32)
    for c in range(n):
        esend[c] = run.astype(BF16)
        run = jnp.broadcast_to(decs[c], (rs, D)) * run + lrec[c].astype(F32)
    erec[me] = esend[me]
    exchange(esend, erec, 2)
    kv_spread()

    def scores(k, masked):
        keys = kv[k, :, 0].reshape(2 * D, D)
        vals = kv[k, :, 1].reshape(2 * D, D)
        for j in range(width // 256):
            lanes = slice(j * 256, (j + 1) * 256)
            s = dot(keys, qt[:, lanes])
            if masked:
                kpos = lax.broadcasted_iota(jnp.int32, (2 * D, 256), 0)
                qpos = core * D + lax.broadcasted_iota(jnp.int32, (2 * D, 256), 1) % D
                s = jnp.where(kpos <= qpos, s, NEG)
            sbuf[k, :, lanes] = s
            m8[:, lanes] = jnp.maximum(m8[:, lanes], jnp.max(s.reshape(2 * D // 8, 8, 256), axis=0))
            dpbuf[k, :, lanes] = dot(vals, ct[:, lanes])

    kv_wait(chip, 1 - core)
    scores(chip, True)

    arrived(erec, 2, n - 1)

    def state(ref, h):
        return ref[h * spn : (h + 1) * spn].reshape(D, D)

    sum_sq = jnp.zeros((D, D), F32)
    sum_x = jnp.zeros((D, D), F32)
    for h in range(H):
        o = out[:, hs(h)] + (SCALE * col(qdec, h)) * dot(lq[:, hs(h)], state(erec, h))
        out[:, hs(h)] = o
        sum_sq += o * o
        sum_x += lc[:, hs(h)].astype(F32) * gain[:, hs(h)] * o
    ones = jnp.ones((8, D), F32)
    pss[0] = dot(ones, sum_sq, 1, 1, HIGH)
    pss[1] = dot(ones, sum_x, 1, 1, HIGH)
    psr[hd] = pss[...]

    @pl.loop(1, nh)
    def _(d):
        to = lax.rem(hd + d, nh)
        pltpu.make_async_remote_copy(
            src_ref=pss,
            dst_ref=psr.at[hd],
            send_sem=a2a_s.at[3],
            recv_sem=a2a_r.at[3],
            device_id={"head": to},
            device_id_type=MESH,
        ).start()

    kv_relay()

    @pl.loop(0, chip // 2)
    def _(i):
        k = chip - 1 - i
        kv_wait(k, 1 - core)
        scores(k, False)

    arrived(psr, 3, nh - 1)
    sums = jnp.sum(psr[...], axis=0)
    inv = lax.rsqrt(sums[0, 0:1] / (nh * width) + EPS)
    cross = sums[1, 0:1] * inv / (nh * width)
    inv_c = column(inv)
    cross_c = column(cross)
    for h in range(H):
        normed = out[:, hs(h)] * inv_c
        cot = lc[:, hs(h)].astype(F32)
        do = ((cot * gain[:, hs(h)] - normed * cross_c) * inv_c).astype(BF16)
        dout[:, hs(h)] = do
        ggs[h : h + 1, :] = jnp.sum(cot * normed, axis=0, keepdims=True)
        qd = (lq[:, hs(h)].astype(F32) * col(qdec, h)).astype(BF16)
        wsend[h * spn : (h + 1) * spn] = dot(qd, do, 0, 0).astype(BF16).reshape(spn, rs, D)
    wrec[me] = wsend[me]
    ggr[me] = ggs[...]
    exchange(wsend, wrec, 4)
    exchange(ggs, ggr, 5, by_target=False)

    for h in range(H):
        do = dout[:, hs(h)]
        dp = (dot(do, lv[:, hs(h)], 1, 1) * ms[h]).astype(BF16)
        o_dq[:, hs(h)] = dot(dp, lk[:, hs(h)]) + (SCALE * col(qdec, h)) * dot(do, state(erec, h), 1, 1)
        o_dk[:, hs(h)] = dot(dp, lq[:, hs(h)], 0, 0)
        o_dv[:, hs(h)] = dot(pw[h], do, 0, 0)

    arrived(wrec, 4, n - 1)
    run = jnp.zeros((rs, D), F32)
    for c in range(n - 1, -1, -1):
        asend[c] = run.astype(BF16)
        run = jnp.broadcast_to(decs[c], (rs, D)) * run + wrec[c].astype(F32)
    arec[me] = asend[me]
    exchange(asend, arec, 6)

    @pl.loop(chip // 2, chip)
    def _(i):
        k = chip - 1 - i
        kv_wait(k, 1 - core)
        scores(k, False)

    factor = SCALE * LOG2E
    top = jnp.max(m8[...], axis=0, keepdims=True) * factor
    l8[...] = jnp.zeros((8, width), F32)
    d8[...] = jnp.zeros((8, width), F32)

    @pl.loop(0, chip + 1)
    def _(k):
        for j in range(width // 256):
            lanes = slice(j * 256, (j + 1) * 256)
            p = jnp.exp2(sbuf[k, :, lanes] * factor - top[:, lanes])
            sbuf[k, :, lanes] = p
            l8[:, lanes] += jnp.sum(p.reshape(2 * D // 8, 8, 256), axis=0)
            d8[:, lanes] += jnp.sum((p * dpbuf[k, :, lanes]).reshape(2 * D // 8, 8, 256), axis=0)

    rinv = 1.0 / jnp.sum(l8[...], axis=0, keepdims=True)
    delta = jnp.sum(d8[...], axis=0, keepdims=True) * rinv
    for h in range(H):
        rc = column(rinv[:, hs(h)])
        qr[h * D : (h + 1) * D, :] = (sq[:, hs(h)].astype(F32) * (rc * SCALE)).astype(BF16)
        cr[h * D : (h + 1) * D, :] = (sc[:, hs(h)].astype(F32) * rc).astype(BF16)

    dqt[...] = jnp.zeros((D, width), F32)

    def pair_copy(k):
        return pltpu.make_async_remote_copy(
            src_ref=pbuf.at[k, 1 - core],
            dst_ref=prec.at[k],
            send_sem=pr_s.at[k],
            recv_sem=pr_r.at[k],
            device_id={"ctx": partner},
            device_id_type=MESH,
        )

    def y_copy(k):
        x, y = k // gy, k % gy
        return pltpu.make_async_remote_copy(
            src_ref=osend.at[k],
            dst_ref=orec.at[x, cy],
            send_sem=os_s.at[k],
            recv_sem=os_r.at[x, cy],
            device_id={"ctx": 2 * (cx * gy + y) + core},
            device_id_type=MESH,
        )

    def x_copy(x):
        return pltpu.make_async_remote_copy(
            src_ref=xsend.at[x],
            dst_ref=xrec.at[cx],
            send_sem=xs_s.at[x],
            recv_sem=xs_r.at[cx],
            device_id={"ctx": 2 * (x * gy + cy) + core},
            device_id_type=MESH,
        )

    def own_send(k):
        pltpu.make_async_copy(prec.at[k], prec.at[k], pr_r.at[k]).wait()
        osend[k] = (pbuf[k, core].astype(F32) + prec[k].astype(F32)).astype(BF16)

        @pl.when(k % gy != cy)
        def _():
            y_copy(k).start()

    @pl.loop(0, chip + 1)
    def _(k):
        keys = kv[k, :, 0].reshape(2 * D, D)
        for j in range(width // 256):
            lanes = slice(j * 256, (j + 1) * 256)
            p = sbuf[k, :, lanes]
            pb[:, lanes] = p.astype(BF16)
            ds = (p * (dpbuf[k, :, lanes] - delta[:, lanes])).astype(BF16)
            dscb[:, lanes] = ds
            dqt[:, lanes] += dot(keys, ds, 0, 0)
        dk = dot(dscb[...], qr[...])
        dv = dot(pb[...], cr[...])
        pbuf[k, :, 0] = dk.astype(BF16).reshape(2, D, D)
        pbuf[k, :, 1] = dv.astype(BF16).reshape(2, D, D)
        pair_copy(k).start()

        @pl.when(k > 0)
        def _():
            own_send(k - 1)

    arrived(arec, 6, n - 1)
    for h in range(H):
        a = state(arec, h)
        kd = SCALE * col(kdec, h)
        o_dk[:, hs(h)] += kd * dot(lv[:, hs(h)], a, 1, 1)
        o_dv[:, hs(h)] += kd * dot(lk[:, hs(h)], a)

    for h in range(H):
        o_sdq[:, hs(h)] = (dqt[:, hs(h)] * (rinv[:, hs(h)] * SCALE)).T

    arrived(ggr, 5, n - 1)
    o_gg[...] = jnp.sum(ggr[...], axis=0)

    def y_add(x, y):
        pltpu.make_async_copy(orec.at[x, y], orec.at[x, y], os_r.at[x, y]).wait()
        acc[...] += orec[x, y].astype(F32)

    @pl.loop(0, cx)
    def _(x):
        acc[...] = osend[x * gy + cy].astype(F32)

        @pl.loop(1, gy)
        def _(d):
            y_add(x, lax.rem(cy + d, gy))

        xsend[x] = acc[...].astype(BF16)
        x_copy(x).start()

    pltpu.make_async_copy(prec.at[chip], prec.at[chip], pr_r.at[chip]).wait()
    acc[...] = pbuf[chip, core].astype(F32) + prec[chip].astype(F32)

    @pl.loop(cy + 1, gy)
    def _(y):
        y_add(cx, y)

    @pl.loop(cx + 1, gx)
    def _(x):
        pltpu.make_async_copy(xrec.at[x], xrec.at[x], xs_r.at[x]).wait()
        acc[...] += xrec[x].astype(F32)

    o_sdk[...] = acc[0]
    o_sdv[...] = acc[1]

    left(lsend, 0, n - 1)
    left(decs, 1, n - 1)
    left(esend, 2, n - 1)
    left(psr, 3, nh - 1)
    left(wsend, 4, n - 1)
    left(ggr, 5, n - 1)
    left(asend, 6, n - 1)

    @pl.loop(0, nc)
    def _(k):
        @pl.when(k <= chip)
        def _():
            pltpu.make_async_copy(kv.at[0, 0], kv.at[0, 0], kv_s.at[k]).wait()

        x, y = k // gy, k % gy
        sent = ((x < cx) & (y != cy)) | ((x == cx) & (y > cy)) | ((x > cx) & (y == cy))

        @pl.when(sent)
        def _():
            pltpu.make_async_copy(kv.at[0, 0], kv.at[0, 0], kv_f.at[k]).wait()

    @pl.loop(0, chip + 1)
    def _(k):
        pltpu.make_async_copy(prec.at[k], prec.at[k], pr_s.at[k]).wait()

    @pl.loop(0, chip)
    def _(k):
        @pl.when(k % gy != cy)
        def _():
            pltpu.make_async_copy(osend.at[k], osend.at[k], os_s.at[k]).wait()

    @pl.loop(0, cx)
    def _(x):
        pltpu.make_async_copy(xsend.at[x], xsend.at[x], xs_s.at[x]).wait()


def finish(*refs):
    copies = [pltpu.make_async_copy(refs[i], refs[7 + i], refs[14].at[i]) for i in range(7)]
    for copy in copies:
        copy.start()
    for copy in copies:
        copy.wait()


def on_device(n, nh, lq, lk, lv, ld, gain, lc, sq, sk, sv, sc):
    nc = n // 2
    gy = math.isqrt(nc)
    gx = nc // gy
    spn = n // H
    rs = D // spn
    width = H * D
    state = pltpu.VMEM((n, rs, D), BF16)
    scratch = [
        pltpu.VMEM((nc, 2 * D, width), F32),
        pltpu.VMEM((nc, 2 * D, width), F32),
        pltpu.VMEM((nc, 2, 2, D, D), BF16),
        pltpu.VMEM((nc, 2, 2, D, D), BF16),
        pltpu.VMEM((nc, 2, D, D), BF16),
        pltpu.VMEM((nc, 2, D, D), BF16),
        pltpu.VMEM((gx, gy, 2, D, D), BF16),
        pltpu.VMEM((gx, 2, D, D), BF16),
        pltpu.VMEM((gx, 2, D, D), BF16),
        pltpu.VMEM((2, D, D), F32),
        pltpu.VMEM((D, width), BF16),
        pltpu.VMEM((D, width), BF16),
        pltpu.VMEM((width, D), BF16),
        pltpu.VMEM((width, D), BF16),
        pltpu.VMEM((2 * D, width), BF16),
        pltpu.VMEM((2 * D, width), BF16),
        pltpu.VMEM((D, width), F32),
        pltpu.VMEM((8, width), F32),
        pltpu.VMEM((8, width), F32),
        pltpu.VMEM((8, width), F32),
        pltpu.VMEM((H, D, D), F32),
        pltpu.VMEM((H, D, D), BF16),
        pltpu.VMEM((D, width), F32),
        pltpu.VMEM((D, width), BF16),
        *([state] * 8),
        pltpu.VMEM((H, 1, D), F32),
        pltpu.VMEM((n, 1, D), F32),
        pltpu.VMEM((H, D), F32),
        pltpu.VMEM((n, H, D), F32),
        pltpu.VMEM((2, 8, D), F32),
        pltpu.VMEM((nh, 2, 8, D), F32),
        pltpu.VMEM((D, width), BF16),
        pltpu.VMEM((D, width), BF16),
        pltpu.VMEM((D, width), BF16),
        pltpu.VMEM((H, D), F32),
        pltpu.VMEM((1, width), F32),
        pltpu.VMEM((D, width), BF16),
        pltpu.VMEM((D, width), BF16),
        pltpu.VMEM((D, width), BF16),
        pltpu.SemaphoreType.DMA((10,)),
        pltpu.SemaphoreType.DMA((7,)),
        pltpu.SemaphoreType.DMA((7,)),
        pltpu.SemaphoreType.DMA((nc,)),
        pltpu.SemaphoreType.DMA((nc,)),
        pltpu.SemaphoreType.DMA((nc, 2)),
        pltpu.SemaphoreType.DMA((nc,)),
        pltpu.SemaphoreType.DMA((nc,)),
        pltpu.SemaphoreType.DMA((nc,)),
        pltpu.SemaphoreType.DMA((gx, gy)),
        pltpu.SemaphoreType.DMA((gx,)),
        pltpu.SemaphoreType.DMA((gx,)),
    ]
    big = pltpu.VMEM((D, width), F32)
    small = pltpu.VMEM((D, D), F32)
    vmem = pl.BlockSpec(memory_space=pltpu.VMEM)
    res = pl.pallas_call(
        functools.partial(kernel, n, nh, gy),
        out_shape=(big, big, big, pltpu.VMEM((H, D), F32), big, small, small),
        in_specs=[pl.BlockSpec(memory_space=pltpu.HBM)] * 10,
        out_specs=(vmem,) * 7,
        scratch_shapes=scratch,
        compiler_params=pltpu.CompilerParams(
            collective_id=0, has_side_effects=True, vmem_limit_bytes=56 * 1024 * 1024
        ),
        name="grads",
    )(lq, lk, lv, ld.T, gain.reshape(1, width), lc, sq, sk, sv, sc)
    dq, dk, dv, gg, sdq, sdk, sdv = pl.pallas_call(
        finish,
        out_shape=tuple(jax.ShapeDtypeStruct(r.shape, r.dtype) for r in res),
        in_specs=[vmem] * 7,
        out_specs=(pl.BlockSpec(memory_space=pl.ANY),) * 7,
        scratch_shapes=[pltpu.SemaphoreType.DMA((7,))],
        compiler_params=pltpu.CompilerParams(vmem_limit_bytes=8 * 1024 * 1024),
        name="finish",
    )(*res)
    return dq, dk, dv, gg.reshape(width), sdq, sdk, sdv


def solution(mesh):
    n, nh = mesh.shape["ctx"], mesh.shape["head"]
    both = P("ctx", "head")
    return jax.shard_map(
        functools.partial(on_device, n, nh),
        mesh=mesh,
        in_specs=(both, both, both, both, P("head"), both, both, both, both, both),
        out_specs=(both, both, both, P("head"), both, both, both),
        check_vma=False,
    )
```

```python
import functools
import math

import jax
import jax.numpy as jnp
from jax import lax
from jax.experimental import pallas as pl
from jax.experimental.pallas import tpu as pltpu
from jax.sharding import PartitionSpec as P

D = 128
H = 8
EPS = 1e-06
NEG = -1e30
SCALE = D**-0.5
LOG2E = math.log2(math.e)
F32 = jnp.float32
BF16 = jnp.bfloat16
HIGH = lax.Precision.HIGHEST
MESH = pl.DeviceIdType.MESH


def dot(a, b, ca=1, cb=0, precision=None):
    return lax.dot_general(
        a, b, (((ca,), (cb,)), ((), ())), precision=precision, preferred_element_type=F32
    )


def hs(h):
    return slice(h * D, (h + 1) * D)


def column(row):
    return jnp.broadcast_to(row, (D, D)).T


def kernel(
    n, nh, gy,
    lq_h, lk_h, lv_h, ld_h, gain_h, lc_h, sq_h, sk_h, sv_h, sc_h,
    o_dq, o_dk, o_dv, o_gg, o_sdq, o_sdk, o_sdv,
    sbuf, dpbuf, kv, pbuf, prec, osend, orec, xsend, xrec, acc,
    qt, ct, qr, cr, dscb, pb, dqt, m8, l8, d8,
    ms, pw, out, dout, lsend, lrec, esend, erec, wsend, wrec, asend, arec,
    dec, decs, ggs, ggr, pss, psr, lq, lk, lv, ld, gain, lc, sq, sc, in_s,
    a2a_s, a2a_r, h_s, h_r, kv_s, kv_f, kv_r, pr_s, pr_r, os_s, os_r, xs_s, xs_r,
):
    me = lax.axis_index("ctx")
    hd = lax.axis_index("head")
    chip = me // 2
    core = me % 2
    partner = me + 1 - 2 * core
    nc = n // 2
    gx = nc // gy
    cx, cy = chip // gy, chip % gy
    spn = n // H
    rs = D // spn
    width = H * D

    loads = [
        pltpu.make_async_copy(a, b, in_s.at[i])
        for i, (a, b) in enumerate(
            [
                (ld_h, ld),
                (lk_h, lk),
                (lv_h, lv),
                (sk_h, kv.at[chip, core, 0]),
                (sv_h, kv.at[chip, core, 1]),
                (lq_h, lq),
                (sq_h, sq),
                (sc_h, sc),
                (lc_h, lc),
                (gain_h, gain),
            ]
        )
    ]
    for load in loads:
        load.start()

    barrier = pltpu.get_barrier_semaphore()

    @pl.loop(1, n)
    def _(d):
        pl.semaphore_signal(
            barrier, inc=1, device_id={"ctx": lax.rem(me + d, n)}, device_id_type=MESH
        )

    @pl.loop(1, nh)
    def _(d):
        pl.semaphore_signal(
            barrier, inc=1, device_id={"head": lax.rem(hd + d, nh)}, device_id_type=MESH
        )

    row_i = lax.broadcasted_iota(jnp.int32, (D, D), 0)
    col_i = lax.broadcasted_iota(jnp.int32, (D, D), 1)
    causal = col_i <= row_i
    tri = jnp.where(causal, 1.0, 0.0).astype(F32)
    loads[0].wait()
    ldv = ld[...]
    cum = dot(tri, ldv, 1, 1, HIGH)
    cum_t = dot(ldv, tri, 1, 1, HIGH)
    kdec = jnp.exp(cum[D - 1 : D, :] - cum)
    qdec = jnp.exp(cum)
    tot_t = jnp.exp(cum_t[:, D - 1 : D])

    def col(a, h):
        return jnp.broadcast_to(a[:, h : h + 1], (D, D))

    loads[1].wait()
    loads[2].wait()
    for h in range(H):
        kd = (lk[:, hs(h)].astype(F32) * col(kdec, h)).astype(BF16)
        local = dot(kd, lv[:, hs(h)], 0, 0)
        lsend[h * spn : (h + 1) * spn] = local.astype(BF16).reshape(spn, rs, D)
        dec[h] = jnp.broadcast_to(tot_t[h : h + 1, :], (1, D))
    lrec[me] = lsend[me]
    decs[me] = dec[me // spn]

    for load in loads[3:]:
        load.wait()
    pl.semaphore_wait(barrier, n - 1 + nh - 1)

    def exchange(src, dst, k, by_target=True, pick=None):
        @pl.loop(1, n)
        def _(d):
            to = lax.rem(me + d, n)
            if pick is not None:
                s = src.at[pick(to)]
            else:
                s = src.at[to] if by_target else src
            pltpu.make_async_remote_copy(
                src_ref=s,
                dst_ref=dst.at[me],
                send_sem=a2a_s.at[k],
                recv_sem=a2a_r.at[k],
                device_id={"ctx": to},
                device_id_type=MESH,
            ).start()

    def arrived(dst, k, count):
        part = dst.at[pl.ds(0, count)]
        pltpu.make_async_copy(part, part, a2a_r.at[k]).wait()

    def left(dst, k, count):
        part = dst.at[pl.ds(0, count)]
        pltpu.make_async_copy(part, part, a2a_s.at[k]).wait()

    half = rs // 2

    def exchange_half(src, dst, k, i):
        rows = pl.ds(i * half, half)

        @pl.loop(1, n)
        def _(d):
            to = lax.rem(me + d, n)
            pltpu.make_async_remote_copy(
                src_ref=src.at[to, rows],
                dst_ref=dst.at[me, rows],
                send_sem=h_s.at[k, i],
                recv_sem=h_r.at[k, i],
                device_id={"ctx": to},
                device_id_type=MESH,
            ).start()

    def half_wait(ref, sem, k, i):
        part = ref.at[pl.ds(0, n - 1), pl.ds(i * half, half)]
        pltpu.make_async_copy(part, part, sem.at[k, i]).wait()

    def scan(src, dst, i, order):
        rows = slice(i * half, (i + 1) * half)
        run = jnp.zeros((half, D), F32)
        for c in order:
            dst[c, rows] = run.astype(BF16)
            run = jnp.broadcast_to(decs[c], (half, D)) * run + src[c, rows].astype(F32)

    exchange(dec, decs, 1, pick=lambda to: to // spn)
    exchange_half(lsend, lrec, 0, 0)
    exchange_half(lsend, lrec, 0, 1)

    def kv_copy(k, sem, to):
        return pltpu.make_async_remote_copy(
            src_ref=kv.at[k, core],
            dst_ref=kv.at[k, core],
            send_sem=sem,
            recv_sem=kv_r.at[k, core],
            device_id={"ctx": to},
            device_id_type=MESH,
        )

    def kv_send():
        kv_copy(chip, kv_s.at[chip], partner).start()

        @pl.loop(cx + 1, gx)
        def _(x):
            k = x * gy + cy
            kv_copy(chip, kv_f.at[k], 2 * k + core).start()

        @pl.loop(cy + 1, gy)
        def _(y):
            k = cx * gy + y
            kv_copy(chip, kv_f.at[k], 2 * k + core).start()

    def kv_spread():
        @pl.loop(0, cx)
        def _(i):
            x = cx - 1 - i
            k = x * gy + cy
            kv_wait(k, core)

            @pl.loop(1, gy)
            def _(d):
                y = lax.rem(cy + d, gy)
                kv_copy(k, kv_f.at[x * gy + y], 2 * (cx * gy + y) + core).start()

            kv_copy(k, kv_s.at[k], partner).start()

    def kv_wait(k, par):
        part = kv.at[k, par]
        pltpu.make_async_copy(part, part, kv_r.at[k, par]).wait()

    def kv_relay():
        @pl.loop(0, chip)
        def _(i):
            k = chip - 1 - i

            @pl.when(k % gy != cy)
            def _():
                kv_wait(k, core)
                kv_copy(k, kv_s.at[k], partner).start()

    kv_send()

    for h in range(H):
        gap = col(cum, h) - jnp.broadcast_to(cum_t[h : h + 1, :], (D, D))
        m = jnp.where(causal, jnp.exp(jnp.minimum(gap, 0.0)), 0.0) * SCALE
        ms[h] = m
        p = (dot(lq[:, hs(h)], lk[:, hs(h)], 1, 1) * m).astype(BF16)
        pw[h] = p
        out[:, hs(h)] = dot(p, lv[:, hs(h)])

    m8[...] = jnp.full((8, width), NEG, F32)
    for h in range(H):
        qh = sq[:, hs(h)]
        chh = sc[:, hs(h)]
        qt[:, hs(h)] = qh.T
        ct[:, hs(h)] = chh.T

    arrived(decs, 1, n - 1)
    for i in range(2):
        half_wait(lrec, h_r, 0, i)
        scan(lrec, esend, i, range(n))
        exchange_half(esend, erec, 1, i)
    erec[me] = esend[me]
    kv_spread()

    def scores(k, masked):
        keys = kv[k, :, 0].reshape(2 * D, D)
        vals = kv[k, :, 1].reshape(2 * D, D)
        for j in range(width // 256):
            lanes = slice(j * 256, (j + 1) * 256)
            s = dot(keys, qt[:, lanes])
            if masked:
                kpos = lax.broadcasted_iota(jnp.int32, (2 * D, 256), 0)
                qpos = core * D + lax.broadcasted_iota(jnp.int32, (2 * D, 256), 1) % D
                s = jnp.where(kpos <= qpos, s, NEG)
            sbuf[k, :, lanes] = s
            m8[:, lanes] = jnp.maximum(m8[:, lanes], jnp.max(s.reshape(2 * D // 8, 8, 256), axis=0))
            dpbuf[k, :, lanes] = dot(vals, ct[:, lanes])

    kv_wait(chip, 1 - core)
    scores(chip, True)

    half_wait(erec, h_r, 1, 0)
    half_wait(erec, h_r, 1, 1)

    def state(ref, h):
        return ref[h * spn : (h + 1) * spn].reshape(D, D)

    sum_sq = jnp.zeros((D, D), F32)
    sum_x = jnp.zeros((D, D), F32)
    for h in range(H):
        o = out[:, hs(h)] + (SCALE * col(qdec, h)) * dot(lq[:, hs(h)], state(erec, h))
        out[:, hs(h)] = o
        sum_sq += o * o
        sum_x += lc[:, hs(h)].astype(F32) * gain[:, hs(h)] * o
    ones = jnp.ones((8, D), F32)
    pss[0] = dot(ones, sum_sq, 1, 1, HIGH)
    pss[1] = dot(ones, sum_x, 1, 1, HIGH)
    psr[hd] = pss[...]

    @pl.loop(1, nh)
    def _(d):
        to = lax.rem(hd + d, nh)
        pltpu.make_async_remote_copy(
            src_ref=pss,
            dst_ref=psr.at[hd],
            send_sem=a2a_s.at[3],
            recv_sem=a2a_r.at[3],
            device_id={"head": to},
            device_id_type=MESH,
        ).start()

    kv_relay()

    @pl.loop(0, chip // 2)
    def _(i):
        k = chip - 1 - i
        kv_wait(k, 1 - core)
        scores(k, False)

    arrived(psr, 3, nh - 1)
    sums = jnp.sum(psr[...], axis=0)
    inv = lax.rsqrt(sums[0, 0:1] / (nh * width) + EPS)
    cross = sums[1, 0:1] * inv / (nh * width)
    inv_c = column(inv)
    cross_c = column(cross)
    for h in range(H):
        normed = out[:, hs(h)] * inv_c
        cot = lc[:, hs(h)].astype(F32)
        do = ((cot * gain[:, hs(h)] - normed * cross_c) * inv_c).astype(BF16)
        dout[:, hs(h)] = do
        ggs[h : h + 1, :] = jnp.sum(cot * normed, axis=0, keepdims=True)
        qd = (lq[:, hs(h)].astype(F32) * col(qdec, h)).astype(BF16)
        wsend[h * spn : (h + 1) * spn] = dot(qd, do, 0, 0).astype(BF16).reshape(spn, rs, D)
    wrec[me] = wsend[me]
    ggr[me] = ggs[...]
    exchange_half(wsend, wrec, 2, 0)
    exchange_half(wsend, wrec, 2, 1)
    exchange(ggs, ggr, 5, by_target=False)

    for h in range(H):
        do = dout[:, hs(h)]
        dp = (dot(do, lv[:, hs(h)], 1, 1) * ms[h]).astype(BF16)
        o_dq[:, hs(h)] = dot(dp, lk[:, hs(h)]) + (SCALE * col(qdec, h)) * dot(do, state(erec, h), 1, 1)
        o_dk[:, hs(h)] = dot(dp, lq[:, hs(h)], 0, 0)
        o_dv[:, hs(h)] = dot(pw[h], do, 0, 0)

    @pl.loop(chip // 2, chip)
    def _(i):
        k = chip - 1 - i
        kv_wait(k, 1 - core)
        scores(k, False)

    for i in range(2):
        half_wait(wrec, h_r, 2, i)
        scan(wrec, asend, i, range(n - 1, -1, -1))
        exchange_half(asend, arec, 3, i)
    arec[me] = asend[me]

    factor = SCALE * LOG2E
    top = jnp.max(m8[...], axis=0, keepdims=True) * factor
    l8[...] = jnp.zeros((8, width), F32)
    d8[...] = jnp.zeros((8, width), F32)

    @pl.loop(0, chip + 1)
    def _(k):
        for j in range(width // 256):
            lanes = slice(j * 256, (j + 1) * 256)
            p = jnp.exp2(sbuf[k, :, lanes] * factor - top[:, lanes])
            sbuf[k, :, lanes] = p
            l8[:, lanes] += jnp.sum(p.reshape(2 * D // 8, 8, 256), axis=0)
            d8[:, lanes] += jnp.sum((p * dpbuf[k, :, lanes]).reshape(2 * D // 8, 8, 256), axis=0)

    rinv = 1.0 / jnp.sum(l8[...], axis=0, keepdims=True)
    delta = jnp.sum(d8[...], axis=0, keepdims=True) * rinv
    for h in range(H):
        rc = column(rinv[:, hs(h)])
        qr[h * D : (h + 1) * D, :] = (sq[:, hs(h)].astype(F32) * (rc * SCALE)).astype(BF16)
        cr[h * D : (h + 1) * D, :] = (sc[:, hs(h)].astype(F32) * rc).astype(BF16)

    dqt[...] = jnp.zeros((D, width), F32)

    def pair_copy(k):
        return pltpu.make_async_remote_copy(
            src_ref=pbuf.at[k, 1 - core],
            dst_ref=prec.at[k],
            send_sem=pr_s.at[k],
            recv_sem=pr_r.at[k],
            device_id={"ctx": partner},
            device_id_type=MESH,
        )

    def y_copy(k):
        x, y = k // gy, k % gy
        return pltpu.make_async_remote_copy(
            src_ref=osend.at[k],
            dst_ref=orec.at[x, cy],
            send_sem=os_s.at[k],
            recv_sem=os_r.at[x, cy],
            device_id={"ctx": 2 * (cx * gy + y) + core},
            device_id_type=MESH,
        )

    def x_copy(x):
        return pltpu.make_async_remote_copy(
            src_ref=xsend.at[x],
            dst_ref=xrec.at[cx],
            send_sem=xs_s.at[x],
            recv_sem=xs_r.at[cx],
            device_id={"ctx": 2 * (x * gy + cy) + core},
            device_id_type=MESH,
        )

    def own_send(k):
        pltpu.make_async_copy(prec.at[k], prec.at[k], pr_r.at[k]).wait()
        osend[k] = (pbuf[k, core].astype(F32) + prec[k].astype(F32)).astype(BF16)

        @pl.when(k % gy != cy)
        def _():
            y_copy(k).start()

    @pl.loop(0, chip + 1)
    def _(k):
        keys = kv[k, :, 0].reshape(2 * D, D)
        for j in range(width // 256):
            lanes = slice(j * 256, (j + 1) * 256)
            p = sbuf[k, :, lanes]
            pb[:, lanes] = p.astype(BF16)
            ds = (p * (dpbuf[k, :, lanes] - delta[:, lanes])).astype(BF16)
            dscb[:, lanes] = ds
            dqt[:, lanes] += dot(keys, ds, 0, 0)
        dk = dot(dscb[...], qr[...])
        dv = dot(pb[...], cr[...])
        pbuf[k, :, 0] = dk.astype(BF16).reshape(2, D, D)
        pbuf[k, :, 1] = dv.astype(BF16).reshape(2, D, D)
        pair_copy(k).start()

        @pl.when(k > 0)
        def _():
            own_send(k - 1)

    half_wait(arec, h_r, 3, 0)
    half_wait(arec, h_r, 3, 1)
    for h in range(H):
        a = state(arec, h)
        kd = SCALE * col(kdec, h)
        o_dk[:, hs(h)] += kd * dot(lv[:, hs(h)], a, 1, 1)
        o_dv[:, hs(h)] += kd * dot(lk[:, hs(h)], a)

    for h in range(H):
        o_sdq[:, hs(h)] = (dqt[:, hs(h)] * (rinv[:, hs(h)] * SCALE)).T

    arrived(ggr, 5, n - 1)
    o_gg[...] = jnp.sum(ggr[...], axis=0)

    def y_add(x, y):
        pltpu.make_async_copy(orec.at[x, y], orec.at[x, y], os_r.at[x, y]).wait()
        acc[...] += orec[x, y].astype(F32)

    @pl.loop(0, cx)
    def _(x):
        acc[...] = osend[x * gy + cy].astype(F32)

        @pl.loop(1, gy)
        def _(d):
            y_add(x, lax.rem(cy + d, gy))

        xsend[x] = acc[...].astype(BF16)
        x_copy(x).start()

    pltpu.make_async_copy(prec.at[chip], prec.at[chip], pr_r.at[chip]).wait()
    acc[...] = pbuf[chip, core].astype(F32) + prec[chip].astype(F32)

    @pl.loop(cy + 1, gy)
    def _(y):
        y_add(cx, y)

    @pl.loop(cx + 1, gx)
    def _(x):
        pltpu.make_async_copy(xrec.at[x], xrec.at[x], xs_r.at[x]).wait()
        acc[...] += xrec[x].astype(F32)

    o_sdk[...] = acc[0]
    o_sdv[...] = acc[1]

    for k, ref in enumerate((lsend, esend, wsend, asend)):
        half_wait(ref, h_s, k, 0)
        half_wait(ref, h_s, k, 1)
    left(decs, 1, n - 1)
    left(psr, 3, nh - 1)
    left(ggr, 5, n - 1)

    @pl.loop(0, nc)
    def _(k):
        @pl.when(k <= chip)
        def _():
            pltpu.make_async_copy(kv.at[0, 0], kv.at[0, 0], kv_s.at[k]).wait()

        x, y = k // gy, k % gy
        sent = ((x < cx) & (y != cy)) | ((x == cx) & (y > cy)) | ((x > cx) & (y == cy))

        @pl.when(sent)
        def _():
            pltpu.make_async_copy(kv.at[0, 0], kv.at[0, 0], kv_f.at[k]).wait()

    @pl.loop(0, chip + 1)
    def _(k):
        pltpu.make_async_copy(prec.at[k], prec.at[k], pr_s.at[k]).wait()

    @pl.loop(0, chip)
    def _(k):
        @pl.when(k % gy != cy)
        def _():
            pltpu.make_async_copy(osend.at[k], osend.at[k], os_s.at[k]).wait()

    @pl.loop(0, cx)
    def _(x):
        pltpu.make_async_copy(xsend.at[x], xsend.at[x], xs_s.at[x]).wait()


def finish(*refs):
    copies = [pltpu.make_async_copy(refs[i], refs[7 + i], refs[14].at[i]) for i in range(7)]
    for copy in copies:
        copy.start()
    for copy in copies:
        copy.wait()


def on_device(n, nh, lq, lk, lv, ld, gain, lc, sq, sk, sv, sc):
    nc = n // 2
    gy = math.isqrt(nc)
    gx = nc // gy
    spn = n // H
    rs = D // spn
    width = H * D
    state = pltpu.VMEM((n, rs, D), BF16)
    scratch = [
        pltpu.VMEM((nc, 2 * D, width), F32),
        pltpu.VMEM((nc, 2 * D, width), F32),
        pltpu.VMEM((nc, 2, 2, D, D), BF16),
        pltpu.VMEM((nc, 2, 2, D, D), BF16),
        pltpu.VMEM((nc, 2, D, D), BF16),
        pltpu.VMEM((nc, 2, D, D), BF16),
        pltpu.VMEM((gx, gy, 2, D, D), BF16),
        pltpu.VMEM((gx, 2, D, D), BF16),
        pltpu.VMEM((gx, 2, D, D), BF16),
        pltpu.VMEM((2, D, D), F32),
        pltpu.VMEM((D, width), BF16),
        pltpu.VMEM((D, width), BF16),
        pltpu.VMEM((width, D), BF16),
        pltpu.VMEM((width, D), BF16),
        pltpu.VMEM((2 * D, width), BF16),
        pltpu.VMEM((2 * D, width), BF16),
        pltpu.VMEM((D, width), F32),
        pltpu.VMEM((8, width), F32),
        pltpu.VMEM((8, width), F32),
        pltpu.VMEM((8, width), F32),
        pltpu.VMEM((H, D, D), F32),
        pltpu.VMEM((H, D, D), BF16),
        pltpu.VMEM((D, width), F32),
        pltpu.VMEM((D, width), BF16),
        *([state] * 8),
        pltpu.VMEM((H, 1, D), F32),
        pltpu.VMEM((n, 1, D), F32),
        pltpu.VMEM((H, D), F32),
        pltpu.VMEM((n, H, D), F32),
        pltpu.VMEM((2, 8, D), F32),
        pltpu.VMEM((nh, 2, 8, D), F32),
        pltpu.VMEM((D, width), BF16),
        pltpu.VMEM((D, width), BF16),
        pltpu.VMEM((D, width), BF16),
        pltpu.VMEM((H, D), F32),
        pltpu.VMEM((1, width), F32),
        pltpu.VMEM((D, width), BF16),
        pltpu.VMEM((D, width), BF16),
        pltpu.VMEM((D, width), BF16),
        pltpu.SemaphoreType.DMA((10,)),
        pltpu.SemaphoreType.DMA((7,)),
        pltpu.SemaphoreType.DMA((7,)),
        pltpu.SemaphoreType.DMA((4, 2)),
        pltpu.SemaphoreType.DMA((4, 2)),
        pltpu.SemaphoreType.DMA((nc,)),
        pltpu.SemaphoreType.DMA((nc,)),
        pltpu.SemaphoreType.DMA((nc, 2)),
        pltpu.SemaphoreType.DMA((nc,)),
        pltpu.SemaphoreType.DMA((nc,)),
        pltpu.SemaphoreType.DMA((nc,)),
        pltpu.SemaphoreType.DMA((gx, gy)),
        pltpu.SemaphoreType.DMA((gx,)),
        pltpu.SemaphoreType.DMA((gx,)),
    ]
    big = pltpu.VMEM((D, width), F32)
    small = pltpu.VMEM((D, D), F32)
    vmem = pl.BlockSpec(memory_space=pltpu.VMEM)
    res = pl.pallas_call(
        functools.partial(kernel, n, nh, gy),
        out_shape=(big, big, big, pltpu.VMEM((H, D), F32), big, small, small),
        in_specs=[pl.BlockSpec(memory_space=pltpu.HBM)] * 10,
        out_specs=(vmem,) * 7,
        scratch_shapes=scratch,
        compiler_params=pltpu.CompilerParams(
            collective_id=0, has_side_effects=True, vmem_limit_bytes=56 * 1024 * 1024
        ),
        name="grads",
    )(lq, lk, lv, ld.T, gain.reshape(1, width), lc, sq, sk, sv, sc)
    dq, dk, dv, gg, sdq, sdk, sdv = pl.pallas_call(
        finish,
        out_shape=tuple(jax.ShapeDtypeStruct(r.shape, r.dtype) for r in res),
        in_specs=[vmem] * 7,
        out_specs=(pl.BlockSpec(memory_space=pl.ANY),) * 7,
        scratch_shapes=[pltpu.SemaphoreType.DMA((7,))],
        compiler_params=pltpu.CompilerParams(vmem_limit_bytes=8 * 1024 * 1024),
        name="finish",
    )(*res)
    return dq, dk, dv, gg.reshape(width), sdq, sdk, sdv


def solution(mesh):
    n, nh = mesh.shape["ctx"], mesh.shape["head"]
    both = P("ctx", "head")
    return jax.shard_map(
        functools.partial(on_device, n, nh),
        mesh=mesh,
        in_specs=(both, both, both, both, P("head"), both, both, both, both, both),
        out_specs=(both, both, both, P("head"), both, both, both),
        check_vma=False,
    )
```

```python
import functools
import math

import jax
import jax.numpy as jnp
from jax import lax
from jax.experimental import pallas as pl
from jax.experimental.pallas import tpu as pltpu
from jax.sharding import PartitionSpec as P

D = 128
H = 8
EPS = 1e-06
NEG = -1e30
SCALE = D**-0.5
LOG2E = math.log2(math.e)
F32 = jnp.float32
BF16 = jnp.bfloat16
HIGH = lax.Precision.HIGHEST
MESH = pl.DeviceIdType.MESH


def dot(a, b, ca=1, cb=0, precision=None):
    return lax.dot_general(
        a, b, (((ca,), (cb,)), ((), ())), precision=precision, preferred_element_type=F32
    )


def hs(h):
    return slice(h * D, (h + 1) * D)


def column(row):
    return jnp.broadcast_to(row, (D, D)).T


def kernel(
    n, nh, gy,
    lq_h, lk_h, lv_h, ld_h, gain_h, lc_h, sq_h, sk_h, sv_h, sc_h,
    o_dq, o_dk, o_dv, o_gg, o_sdq, o_sdk, o_sdv,
    sbuf, dpbuf, kv, pbuf, prec, osend, orec, xsend, xrec, acc,
    qt, ct, qr, cr, dscb, pb, dqt, m8, l8, d8,
    ms, pw, out, dout, lsend, lrec, esend, erec, wsend, wrec, asend, arec,
    dec, decs, ggs, ggr, pss, psr, lq, lk, lv, ld, gain, lc, sq, sc, in_s,
    a2a_s, a2a_r, h_s, h_r, kv_s, kv_f, kv_r, pr_s, pr_r, os_s, os_r, xs_s, xs_r,
):
    me = lax.axis_index("ctx")
    hd = lax.axis_index("head")
    chip = me // 2
    core = me % 2
    partner = me + 1 - 2 * core
    nc = n // 2
    gx = nc // gy
    cx, cy = chip // gy, chip % gy
    spn = n // H
    rs = D // spn
    width = H * D

    loads = [
        pltpu.make_async_copy(a, b, in_s.at[i])
        for i, (a, b) in enumerate(
            [
                (ld_h, ld),
                (lk_h, lk),
                (lv_h, lv),
                (sk_h, kv.at[chip, core, 0]),
                (sv_h, kv.at[chip, core, 1]),
                (lq_h, lq),
                (sq_h, sq),
                (sc_h, sc),
                (lc_h, lc),
                (gain_h, gain),
            ]
        )
    ]
    for load in loads:
        load.start()

    barrier = pltpu.get_barrier_semaphore()

    @pl.loop(1, n)
    def _(d):
        pl.semaphore_signal(
            barrier, inc=1, device_id={"ctx": lax.rem(me + d, n)}, device_id_type=MESH
        )

    @pl.loop(1, nh)
    def _(d):
        pl.semaphore_signal(
            barrier, inc=1, device_id={"head": lax.rem(hd + d, nh)}, device_id_type=MESH
        )

    row_i = lax.broadcasted_iota(jnp.int32, (D, D), 0)
    col_i = lax.broadcasted_iota(jnp.int32, (D, D), 1)
    causal = col_i <= row_i
    tri = jnp.where(causal, 1.0, 0.0).astype(F32)
    loads[0].wait()
    ldv = ld[...]
    cum = dot(tri, ldv, 1, 1, HIGH)
    cum_t = dot(ldv, tri, 1, 1, HIGH)
    kdec = jnp.exp(cum[D - 1 : D, :] - cum)
    qdec = jnp.exp(cum)
    tot_t = jnp.exp(cum_t[:, D - 1 : D])

    def col(a, h):
        return jnp.broadcast_to(a[:, h : h + 1], (D, D))

    loads[1].wait()
    loads[2].wait()
    for h in range(H):
        kd = (lk[:, hs(h)].astype(F32) * col(kdec, h)).astype(BF16)
        local = dot(kd, lv[:, hs(h)], 0, 0)
        lsend[h * spn : (h + 1) * spn] = local.astype(BF16).reshape(spn, rs, D)
        dec[h] = jnp.broadcast_to(tot_t[h : h + 1, :], (1, D))
    lrec[me] = lsend[me]
    decs[me] = dec[me // spn]

    for load in loads[3:]:
        load.wait()
    pl.semaphore_wait(barrier, n - 1 + nh - 1)

    def exchange(src, dst, k, by_target=True, pick=None):
        @pl.loop(1, n)
        def _(d):
            to = lax.rem(me + d, n)
            if pick is not None:
                s = src.at[pick(to)]
            else:
                s = src.at[to] if by_target else src
            pltpu.make_async_remote_copy(
                src_ref=s,
                dst_ref=dst.at[me],
                send_sem=a2a_s.at[k],
                recv_sem=a2a_r.at[k],
                device_id={"ctx": to},
                device_id_type=MESH,
            ).start()

    def arrived(dst, k, count):
        part = dst.at[pl.ds(0, count)]
        pltpu.make_async_copy(part, part, a2a_r.at[k]).wait()

    def left(dst, k, count):
        part = dst.at[pl.ds(0, count)]
        pltpu.make_async_copy(part, part, a2a_s.at[k]).wait()

    half = rs // 2

    def exchange_half(src, dst, k, i):
        rows = pl.ds(i * half, half)

        @pl.loop(1, n)
        def _(d):
            to = lax.rem(me + d, n)
            pltpu.make_async_remote_copy(
                src_ref=src.at[to, rows],
                dst_ref=dst.at[me, rows],
                send_sem=h_s.at[k, i],
                recv_sem=h_r.at[k, i],
                device_id={"ctx": to},
                device_id_type=MESH,
            ).start()

    def half_wait(ref, sem, k, i):
        part = ref.at[pl.ds(0, n - 1), pl.ds(i * half, half)]
        pltpu.make_async_copy(part, part, sem.at[k, i]).wait()

    def scan(src, dst, i, order):
        rows = slice(i * half, (i + 1) * half)
        run = jnp.zeros((half, D), F32)
        for c in order:
            dst[c, rows] = run.astype(BF16)
            run = jnp.broadcast_to(decs[c], (half, D)) * run + src[c, rows].astype(F32)

    exchange(dec, decs, 1, pick=lambda to: to // spn)
    exchange_half(lsend, lrec, 0, 0)
    exchange_half(lsend, lrec, 0, 1)

    def kv_copy(k, sem, to):
        return pltpu.make_async_remote_copy(
            src_ref=kv.at[k, core],
            dst_ref=kv.at[k, core],
            send_sem=sem,
            recv_sem=kv_r.at[k, core],
            device_id={"ctx": to},
            device_id_type=MESH,
        )

    def kv_send():
        kv_copy(chip, kv_s.at[chip], partner).start()

        @pl.loop(cx + 1, gx)
        def _(x):
            k = x * gy + cy
            kv_copy(chip, kv_f.at[k], 2 * k + core).start()

        @pl.loop(cy + 1, gy)
        def _(y):
            k = cx * gy + y
            kv_copy(chip, kv_f.at[k], 2 * k + core).start()

    def kv_spread():
        @pl.loop(0, cx)
        def _(i):
            x = cx - 1 - i
            k = x * gy + cy
            kv_wait(k, core)

            @pl.loop(1, gy)
            def _(d):
                y = lax.rem(cy + d, gy)
                kv_copy(k, kv_f.at[x * gy + y], 2 * (cx * gy + y) + core).start()

            kv_copy(k, kv_s.at[k], partner).start()

    def kv_wait(k, par):
        part = kv.at[k, par]
        pltpu.make_async_copy(part, part, kv_r.at[k, par]).wait()

    def kv_relay():
        @pl.loop(0, chip)
        def _(i):
            k = chip - 1 - i

            @pl.when(k % gy != cy)
            def _():
                kv_wait(k, core)
                kv_copy(k, kv_s.at[k], partner).start()

    kv_send()

    for h in range(H):
        gap = col(cum, h) - jnp.broadcast_to(cum_t[h : h + 1, :], (D, D))
        m = jnp.where(causal, jnp.exp(jnp.minimum(gap, 0.0)), 0.0) * SCALE
        ms[h] = m
        p = (dot(lq[:, hs(h)], lk[:, hs(h)], 1, 1) * m).astype(BF16)
        pw[h] = p
        out[:, hs(h)] = dot(p, lv[:, hs(h)])

    m8[...] = jnp.full((8, width), NEG, F32)
    for h in range(H):
        qh = sq[:, hs(h)]
        chh = sc[:, hs(h)]
        qt[:, hs(h)] = qh.T
        ct[:, hs(h)] = chh.T

    arrived(decs, 1, n - 1)
    for i in range(2):
        half_wait(lrec, h_r, 0, i)
        scan(lrec, esend, i, range(n))
        exchange_half(esend, erec, 1, i)
    erec[me] = esend[me]
    kv_spread()

    def scores(k, masked):
        keys = kv[k, :, 0].reshape(2 * D, D)
        vals = kv[k, :, 1].reshape(2 * D, D)
        for j in range(width // 256):
            lanes = slice(j * 256, (j + 1) * 256)
            s = dot(keys, qt[:, lanes])
            if masked:
                kpos = lax.broadcasted_iota(jnp.int32, (2 * D, 256), 0)
                qpos = core * D + lax.broadcasted_iota(jnp.int32, (2 * D, 256), 1) % D
                s = jnp.where(kpos <= qpos, s, NEG)
            sbuf[k, :, lanes] = s
            m8[:, lanes] = jnp.maximum(m8[:, lanes], jnp.max(s.reshape(2 * D // 8, 8, 256), axis=0))
            dpbuf[k, :, lanes] = dot(vals, ct[:, lanes])

    kv_wait(chip, 1 - core)
    scores(chip, True)

    half_wait(erec, h_r, 1, 0)
    half_wait(erec, h_r, 1, 1)

    def state(ref, h):
        return ref[h * spn : (h + 1) * spn].reshape(D, D)

    sum_sq = jnp.zeros((D, D), F32)
    sum_x = jnp.zeros((D, D), F32)
    for h in range(H):
        o = out[:, hs(h)] + (SCALE * col(qdec, h)) * dot(lq[:, hs(h)], state(erec, h))
        out[:, hs(h)] = o
        sum_sq += o * o
        sum_x += lc[:, hs(h)].astype(F32) * gain[:, hs(h)] * o
    ones = jnp.ones((8, D), F32)
    pss[0] = dot(ones, sum_sq, 1, 1, HIGH)
    pss[1] = dot(ones, sum_x, 1, 1, HIGH)
    psr[hd] = pss[...]

    @pl.loop(1, nh)
    def _(d):
        to = lax.rem(hd + d, nh)
        pltpu.make_async_remote_copy(
            src_ref=pss,
            dst_ref=psr.at[hd],
            send_sem=a2a_s.at[3],
            recv_sem=a2a_r.at[3],
            device_id={"head": to},
            device_id_type=MESH,
        ).start()

    arrived(psr, 3, nh - 1)
    sums = jnp.sum(psr[...], axis=0)
    inv = lax.rsqrt(sums[0, 0:1] / (nh * width) + EPS)
    cross = sums[1, 0:1] * inv / (nh * width)
    inv_c = column(inv)
    cross_c = column(cross)
    for h in range(H):
        normed = out[:, hs(h)] * inv_c
        cot = lc[:, hs(h)].astype(F32)
        do = ((cot * gain[:, hs(h)] - normed * cross_c) * inv_c).astype(BF16)
        dout[:, hs(h)] = do
        ggs[h : h + 1, :] = jnp.sum(cot * normed, axis=0, keepdims=True)
        qd = (lq[:, hs(h)].astype(F32) * col(qdec, h)).astype(BF16)
        wsend[h * spn : (h + 1) * spn] = dot(qd, do, 0, 0).astype(BF16).reshape(spn, rs, D)
    wrec[me] = wsend[me]
    ggr[me] = ggs[...]
    exchange_half(wsend, wrec, 2, 0)
    exchange_half(wsend, wrec, 2, 1)
    exchange(ggs, ggr, 5, by_target=False)

    for h in range(H):
        do = dout[:, hs(h)]
        dp = (dot(do, lv[:, hs(h)], 1, 1) * ms[h]).astype(BF16)
        o_dq[:, hs(h)] = dot(dp, lk[:, hs(h)]) + (SCALE * col(qdec, h)) * dot(do, state(erec, h), 1, 1)
        o_dk[:, hs(h)] = dot(dp, lq[:, hs(h)], 0, 0)
        o_dv[:, hs(h)] = dot(pw[h], do, 0, 0)

    kv_relay()

    @pl.loop(0, chip)
    def _(i):
        k = chip - 1 - i
        kv_wait(k, 1 - core)
        scores(k, False)

    for i in range(2):
        half_wait(wrec, h_r, 2, i)
        scan(wrec, asend, i, range(n - 1, -1, -1))
        exchange_half(asend, arec, 3, i)
    arec[me] = asend[me]

    factor = SCALE * LOG2E
    top = jnp.max(m8[...], axis=0, keepdims=True) * factor
    l8[...] = jnp.zeros((8, width), F32)
    d8[...] = jnp.zeros((8, width), F32)

    @pl.loop(0, chip + 1)
    def _(k):
        for j in range(width // 256):
            lanes = slice(j * 256, (j + 1) * 256)
            p = jnp.exp2(sbuf[k, :, lanes] * factor - top[:, lanes])
            sbuf[k, :, lanes] = p
            l8[:, lanes] += jnp.sum(p.reshape(2 * D // 8, 8, 256), axis=0)
            d8[:, lanes] += jnp.sum((p * dpbuf[k, :, lanes]).reshape(2 * D // 8, 8, 256), axis=0)

    rinv = 1.0 / jnp.sum(l8[...], axis=0, keepdims=True)
    delta = jnp.sum(d8[...], axis=0, keepdims=True) * rinv
    for h in range(H):
        rc = column(rinv[:, hs(h)])
        qr[h * D : (h + 1) * D, :] = (sq[:, hs(h)].astype(F32) * (rc * SCALE)).astype(BF16)
        cr[h * D : (h + 1) * D, :] = (sc[:, hs(h)].astype(F32) * rc).astype(BF16)

    dqt[...] = jnp.zeros((D, width), F32)

    def pair_copy(k):
        return pltpu.make_async_remote_copy(
            src_ref=pbuf.at[k, 1 - core],
            dst_ref=prec.at[k],
            send_sem=pr_s.at[k],
            recv_sem=pr_r.at[k],
            device_id={"ctx": partner},
            device_id_type=MESH,
        )

    def y_copy(k):
        x, y = k // gy, k % gy
        return pltpu.make_async_remote_copy(
            src_ref=osend.at[k],
            dst_ref=orec.at[x, cy],
            send_sem=os_s.at[k],
            recv_sem=os_r.at[x, cy],
            device_id={"ctx": 2 * (cx * gy + y) + core},
            device_id_type=MESH,
        )

    def x_copy(x):
        return pltpu.make_async_remote_copy(
            src_ref=xsend.at[x],
            dst_ref=xrec.at[cx],
            send_sem=xs_s.at[x],
            recv_sem=xs_r.at[cx],
            device_id={"ctx": 2 * (x * gy + cy) + core},
            device_id_type=MESH,
        )

    def own_send(k):
        pltpu.make_async_copy(prec.at[k], prec.at[k], pr_r.at[k]).wait()
        osend[k] = (pbuf[k, core].astype(F32) + prec[k].astype(F32)).astype(BF16)

        @pl.when(k % gy != cy)
        def _():
            y_copy(k).start()

    @pl.loop(0, chip + 1)
    def _(k):
        keys = kv[k, :, 0].reshape(2 * D, D)
        for j in range(width // 256):
            lanes = slice(j * 256, (j + 1) * 256)
            p = sbuf[k, :, lanes]
            pb[:, lanes] = p.astype(BF16)
            ds = (p * (dpbuf[k, :, lanes] - delta[:, lanes])).astype(BF16)
            dscb[:, lanes] = ds
            dqt[:, lanes] += dot(keys, ds, 0, 0)
        dk = dot(dscb[...], qr[...])
        dv = dot(pb[...], cr[...])
        pbuf[k, :, 0] = dk.astype(BF16).reshape(2, D, D)
        pbuf[k, :, 1] = dv.astype(BF16).reshape(2, D, D)
        pair_copy(k).start()

        @pl.when(k > 0)
        def _():
            own_send(k - 1)

    half_wait(arec, h_r, 3, 0)
    half_wait(arec, h_r, 3, 1)
    for h in range(H):
        a = state(arec, h)
        kd = SCALE * col(kdec, h)
        o_dk[:, hs(h)] += kd * dot(lv[:, hs(h)], a, 1, 1)
        o_dv[:, hs(h)] += kd * dot(lk[:, hs(h)], a)

    for h in range(H):
        o_sdq[:, hs(h)] = (dqt[:, hs(h)] * (rinv[:, hs(h)] * SCALE)).T

    arrived(ggr, 5, n - 1)
    o_gg[...] = jnp.sum(ggr[...], axis=0)

    def y_add(x, y):
        pltpu.make_async_copy(orec.at[x, y], orec.at[x, y], os_r.at[x, y]).wait()
        acc[...] += orec[x, y].astype(F32)

    @pl.loop(0, cx)
    def _(x):
        acc[...] = osend[x * gy + cy].astype(F32)

        @pl.loop(1, gy)
        def _(d):
            y_add(x, lax.rem(cy + d, gy))

        xsend[x] = acc[...].astype(BF16)
        x_copy(x).start()

    pltpu.make_async_copy(prec.at[chip], prec.at[chip], pr_r.at[chip]).wait()
    acc[...] = pbuf[chip, core].astype(F32) + prec[chip].astype(F32)

    @pl.loop(cy + 1, gy)
    def _(y):
        y_add(cx, y)

    @pl.loop(cx + 1, gx)
    def _(x):
        pltpu.make_async_copy(xrec.at[x], xrec.at[x], xs_r.at[x]).wait()
        acc[...] += xrec[x].astype(F32)

    o_sdk[...] = acc[0]
    o_sdv[...] = acc[1]

    for k, ref in enumerate((lsend, esend, wsend, asend)):
        half_wait(ref, h_s, k, 0)
        half_wait(ref, h_s, k, 1)
    left(decs, 1, n - 1)
    left(psr, 3, nh - 1)
    left(ggr, 5, n - 1)

    @pl.loop(0, nc)
    def _(k):
        @pl.when(k <= chip)
        def _():
            pltpu.make_async_copy(kv.at[0, 0], kv.at[0, 0], kv_s.at[k]).wait()

        x, y = k // gy, k % gy
        sent = ((x < cx) & (y != cy)) | ((x == cx) & (y > cy)) | ((x > cx) & (y == cy))

        @pl.when(sent)
        def _():
            pltpu.make_async_copy(kv.at[0, 0], kv.at[0, 0], kv_f.at[k]).wait()

    @pl.loop(0, chip + 1)
    def _(k):
        pltpu.make_async_copy(prec.at[k], prec.at[k], pr_s.at[k]).wait()

    @pl.loop(0, chip)
    def _(k):
        @pl.when(k % gy != cy)
        def _():
            pltpu.make_async_copy(osend.at[k], osend.at[k], os_s.at[k]).wait()

    @pl.loop(0, cx)
    def _(x):
        pltpu.make_async_copy(xsend.at[x], xsend.at[x], xs_s.at[x]).wait()


def finish(*refs):
    copies = [pltpu.make_async_copy(refs[i], refs[7 + i], refs[14].at[i]) for i in range(7)]
    for copy in copies:
        copy.start()
    for copy in copies:
        copy.wait()


def on_device(n, nh, lq, lk, lv, ld, gain, lc, sq, sk, sv, sc):
    nc = n // 2
    gy = math.isqrt(nc)
    gx = nc // gy
    spn = n // H
    rs = D // spn
    width = H * D
    state = pltpu.VMEM((n, rs, D), BF16)
    scratch = [
        pltpu.VMEM((nc, 2 * D, width), F32),
        pltpu.VMEM((nc, 2 * D, width), F32),
        pltpu.VMEM((nc, 2, 2, D, D), BF16),
        pltpu.VMEM((nc, 2, 2, D, D), BF16),
        pltpu.VMEM((nc, 2, D, D), BF16),
        pltpu.VMEM((nc, 2, D, D), BF16),
        pltpu.VMEM((gx, gy, 2, D, D), BF16),
        pltpu.VMEM((gx, 2, D, D), BF16),
        pltpu.VMEM((gx, 2, D, D), BF16),
        pltpu.VMEM((2, D, D), F32),
        pltpu.VMEM((D, width), BF16),
        pltpu.VMEM((D, width), BF16),
        pltpu.VMEM((width, D), BF16),
        pltpu.VMEM((width, D), BF16),
        pltpu.VMEM((2 * D, width), BF16),
        pltpu.VMEM((2 * D, width), BF16),
        pltpu.VMEM((D, width), F32),
        pltpu.VMEM((8, width), F32),
        pltpu.VMEM((8, width), F32),
        pltpu.VMEM((8, width), F32),
        pltpu.VMEM((H, D, D), F32),
        pltpu.VMEM((H, D, D), BF16),
        pltpu.VMEM((D, width), F32),
        pltpu.VMEM((D, width), BF16),
        *([state] * 8),
        pltpu.VMEM((H, 1, D), F32),
        pltpu.VMEM((n, 1, D), F32),
        pltpu.VMEM((H, D), F32),
        pltpu.VMEM((n, H, D), F32),
        pltpu.VMEM((2, 8, D), F32),
        pltpu.VMEM((nh, 2, 8, D), F32),
        pltpu.VMEM((D, width), BF16),
        pltpu.VMEM((D, width), BF16),
        pltpu.VMEM((D, width), BF16),
        pltpu.VMEM((H, D), F32),
        pltpu.VMEM((1, width), F32),
        pltpu.VMEM((D, width), BF16),
        pltpu.VMEM((D, width), BF16),
        pltpu.VMEM((D, width), BF16),
        pltpu.SemaphoreType.DMA((10,)),
        pltpu.SemaphoreType.DMA((7,)),
        pltpu.SemaphoreType.DMA((7,)),
        pltpu.SemaphoreType.DMA((4, 2)),
        pltpu.SemaphoreType.DMA((4, 2)),
        pltpu.SemaphoreType.DMA((nc,)),
        pltpu.SemaphoreType.DMA((nc,)),
        pltpu.SemaphoreType.DMA((nc, 2)),
        pltpu.SemaphoreType.DMA((nc,)),
        pltpu.SemaphoreType.DMA((nc,)),
        pltpu.SemaphoreType.DMA((nc,)),
        pltpu.SemaphoreType.DMA((gx, gy)),
        pltpu.SemaphoreType.DMA((gx,)),
        pltpu.SemaphoreType.DMA((gx,)),
    ]
    big = pltpu.VMEM((D, width), F32)
    small = pltpu.VMEM((D, D), F32)
    vmem = pl.BlockSpec(memory_space=pltpu.VMEM)
    res = pl.pallas_call(
        functools.partial(kernel, n, nh, gy),
        out_shape=(big, big, big, pltpu.VMEM((H, D), F32), big, small, small),
        in_specs=[pl.BlockSpec(memory_space=pltpu.HBM)] * 10,
        out_specs=(vmem,) * 7,
        scratch_shapes=scratch,
        compiler_params=pltpu.CompilerParams(
            collective_id=0, has_side_effects=True, vmem_limit_bytes=56 * 1024 * 1024
        ),
        name="grads",
    )(lq, lk, lv, ld.T, gain.reshape(1, width), lc, sq, sk, sv, sc)
    dq, dk, dv, gg, sdq, sdk, sdv = pl.pallas_call(
        finish,
        out_shape=tuple(jax.ShapeDtypeStruct(r.shape, r.dtype) for r in res),
        in_specs=[vmem] * 7,
        out_specs=(pl.BlockSpec(memory_space=pl.ANY),) * 7,
        scratch_shapes=[pltpu.SemaphoreType.DMA((7,))],
        compiler_params=pltpu.CompilerParams(vmem_limit_bytes=8 * 1024 * 1024),
        name="finish",
    )(*res)
    return dq, dk, dv, gg.reshape(width), sdq, sdk, sdv


def solution(mesh):
    n, nh = mesh.shape["ctx"], mesh.shape["head"]
    both = P("ctx", "head")
    return jax.shard_map(
        functools.partial(on_device, n, nh),
        mesh=mesh,
        in_specs=(both, both, both, both, P("head"), both, both, both, both, both),
        out_specs=(both, both, both, P("head"), both, both, both),
        check_vma=False,
    )
```
